256 devices in a mesh: seq: 64 (over x, z, core), rep: 4 (over y).
Axes of the slice: x: 4, y: 4, z: 8, core: 2. Of those that a mesh axis runs over, the one named last changes fastest.
Arguments:
- query_in: bfloat16 [4, 8192, 1024], P('rep', 'seq'), may hold values from -120 to 120
- key_in: bfloat16 [4, 8192, 1024], P('rep', 'seq'), may hold values from -4 to 4
- value_in: bfloat16 [4, 8192, 1024], P('rep', 'seq'), may hold values from -6 to 6
- out_weight: bfloat16 [1024, 2048], replicated, may hold values from -0.1875 to 0.1875
- grad_out: bfloat16 [4, 8192, 2048], P('rep', 'seq'), may hold values from -6 to 6
- pattern: int32 [128, 8], replicated, may hold values from 0 to 127, as said below
Outputs:
- mixed_out: bfloat16 [4, 8192, 2048], P('rep', 'seq')
- query_grad: bfloat16 [4, 8192, 1024], P('rep', 'seq')
- key_grad: bfloat16 [4, 8192, 1024], P('rep', 'seq')
- value_grad: bfloat16 [4, 8192, 1024], P('rep', 'seq')
- weight_grad: float32 [1024, 2048], P('seq')
The draws below stay inside these ranges and needn't reach their ends.
Inputs may be any that keep to these rules, and one draw needn't show every extreme that they name: `pattern`: row b names blocks b - 1, b and b + 1 modulo 128 in columns 0 to 2; columns 3 and 4 hold the same two blocks in every row; the other columns may name any block.
All inputs are finite; a program needn't handle non-finite values.
Results may differ from the reference program's by a relative error of at most 0.0095.
Values may be sent and summed in bfloat16 or wider, within the bound.
A program may use at most 128 MiB of HBM per device.

```python
import math
import jax
import jax.numpy as jnp
from jax import lax

HD = 128
HEADS = 8
D = 2048
BLK = 64
R = 8
DOCS = 4
TOKENS = 8192
NB = 128
GROUPS = 8


def draw_key_in(key, part):
    result = jnp.clip(jax.random.normal(jax.random.fold_in(key, 21), (DOCS, TOKENS, HEADS * HD), jnp.float32), -4.0, 4.0)
    return result.astype(jnp.bfloat16)


def draw_query_in(key, part):
    result = jnp.clip(jax.random.normal(jax.random.fold_in(key, 22), (DOCS, TOKENS, HEADS * HD), jnp.float32), -4.0, 4.0)
    return result.astype(jnp.bfloat16)


def draw_pattern(key, part):
    blocks = jnp.arange(NB, dtype=jnp.int32)
    window = jnp.stack([(blocks + NB - 1) % NB, blocks, (blocks + 1) % NB], axis=1)
    global_ids = jax.random.randint(jax.random.fold_in(key, 31), (1, 2), 0, NB, dtype=jnp.int32)
    global_cols = jnp.broadcast_to(global_ids, (NB, 2))
    random_cols = jax.random.randint(jax.random.fold_in(key, 32), (NB, R - 5), 0, NB, dtype=jnp.int32)
    return jnp.concatenate([window, global_cols, random_cols], axis=1).astype(jnp.int32)


def steps_of(stream_key, shape, split, least, top_value):
    gain, own = 1.0, jax.random.fold_in(stream_key, 6)
    for position, blocks in split:
        draws = jnp.exp(jax.random.uniform(jax.random.fold_in(own, position), (blocks,), jnp.float32, least / len(split), top_value / len(split)))
        gain = gain * jnp.repeat(draws, shape[position] // blocks).reshape([-1 if axis == position else 1 for axis in range(len(shape))])
    return gain


def bell_draw(rng, extent, scale, bound, split=(), kind=jnp.bfloat16):
    values = jax.random.normal(rng, extent, jnp.float32) * scale
    if len(split) > 0:
        values = steps_of(rng, extent, split, -0.22, 0.18) * values
    return jnp.clip(values, min=-bound, max=bound).astype(kind)


def setup_inputs(seed: int = 0) -> dict:
    key_of = jax.random.split(jax.random.key(seed), 7)
    return {
        "query_in": draw_query_in(jax.random.fold_in(key_of[6], 71), 0),
        "key_in": draw_key_in(jax.random.fold_in(key_of[6], 71), 0),
        "value_in": bell_draw(key_of[2], (DOCS, TOKENS, HEADS * HD), 1.0, 6.0, ((0, 4), (1, 64))),
        "out_weight": bell_draw(key_of[3], (HEADS * HD, D), (HEADS * HD) ** -0.5, 0.1875),
        "grad_out": bell_draw(key_of[4], (DOCS, TOKENS, D), 1.0, 6.0, ((0, 4), (1, 64))),
        "pattern": draw_pattern(jax.random.fold_in(key_of[6], 71), 0),
    }


def gather_blocks(blocks, pattern):
    return blocks[pattern].reshape(NB, R * BLK, HD)

def softmax_rows(queries, gathered):
    scores = jnp.einsum('nqd,nkd->nqk', queries.astype(jnp.float32), gathered.astype(jnp.float32)) * (1.0 / math.sqrt(HD))
    shifted = scores - lax.optimization_barrier(jnp.max(scores, axis=-1, keepdims=True))
    weights = jnp.exp(shifted)
    return weights / lax.optimization_barrier(jnp.sum(weights, axis=-1, keepdims=True))

def head_forward(queries, keys_head, values_head, pattern):
    key_gathered = gather_blocks(keys_head, pattern)
    value_gathered = gather_blocks(values_head, pattern)
    probs = softmax_rows(queries, key_gathered)
    probs_low = probs.astype(jnp.bfloat16)
    result = jnp.einsum('nqk,nkd->nqd', probs_low.astype(jnp.float32), value_gathered.astype(jnp.float32))
    return result.astype(jnp.bfloat16)

def round_sum(parts):
    rounded = lax.optimization_barrier(parts.astype(jnp.bfloat16))
    return lax.optimization_barrier(jnp.sum(rounded.astype(jnp.float32), axis=0)).astype(jnp.bfloat16)

def scatter_parts(contrib, pattern):
    shaped = contrib.reshape(GROUPS, NB, R, BLK, HD)
    return jnp.zeros((GROUPS, NB, BLK, HD), jnp.float32).at[:, pattern].add(shaped)

def head_backward(queries, keys_head, values_head, out_grad, pattern):
    scale = 1.0 / math.sqrt(HD)
    key_gathered = gather_blocks(keys_head, pattern)
    value_gathered = gather_blocks(values_head, pattern)
    probs = softmax_rows(queries, key_gathered)
    probs_low = probs.astype(jnp.bfloat16)
    prob_grad = jnp.einsum('nqd,nkd->nqk', out_grad.astype(jnp.float32), value_gathered.astype(jnp.float32))
    delta = lax.optimization_barrier(jnp.sum(probs * prob_grad, axis=-1, keepdims=True))
    score_grad = (probs * (prob_grad - delta)).astype(jnp.bfloat16)
    query_part = jnp.einsum('nqk,nkd->nqd', score_grad.astype(jnp.float32), key_gathered.astype(jnp.float32)) * scale
    group_rows = BLK // GROUPS
    score_groups = score_grad.reshape(NB, GROUPS, group_rows, R * BLK).astype(jnp.float32)
    query_groups = queries.reshape(NB, GROUPS, group_rows, HD).astype(jnp.float32)
    prob_groups = probs_low.reshape(NB, GROUPS, group_rows, R * BLK).astype(jnp.float32)
    grad_groups = out_grad.reshape(NB, GROUPS, group_rows, HD).astype(jnp.float32)
    key_contrib = jnp.einsum('ngqk,ngqd->gnkd', score_groups, query_groups) * scale
    value_contrib = jnp.einsum('ngqk,ngqd->gnkd', prob_groups, grad_groups)
    key_total = round_sum(scatter_parts(key_contrib, pattern))
    value_total = round_sum(scatter_parts(value_contrib, pattern))
    return (query_part.astype(jnp.bfloat16), key_total, value_total)

def split_heads(source):
    return source.reshape(DOCS, NB, BLK, HEADS, HD).transpose(0, 3, 1, 2, 4).reshape(DOCS * HEADS, NB, BLK, HD)

def merge_heads(source):
    return source.reshape(DOCS, HEADS, NB, BLK, HD).transpose(0, 2, 3, 1, 4).reshape(DOCS, TOKENS, HEADS * HD)

def reference(query_in, key_in, value_in, out_weight, grad_out, pattern):
    query_split = split_heads(query_in)
    key_split = split_heads(key_in)
    value_split = split_heads(value_in)
    attended = merge_heads(lax.map(lambda items: head_forward(items[0], items[1], items[2], pattern), (query_split, key_split, value_split)))
    flat_attended = attended.reshape(DOCS * TOKENS, HEADS * HD)
    flat_grad = grad_out.reshape(DOCS * TOKENS, D)
    mixed_out = jnp.dot(flat_attended, out_weight, preferred_element_type=jnp.float32).astype(jnp.bfloat16).reshape(DOCS, TOKENS, D)
    attended_grad = jnp.dot(flat_grad, out_weight.T, preferred_element_type=jnp.float32).astype(jnp.bfloat16)
    weight_grad = jnp.dot(flat_attended.T, flat_grad, preferred_element_type=jnp.float32) * (1.0 / math.sqrt(DOCS * TOKENS))
    grad_split = split_heads(attended_grad.reshape(DOCS, TOKENS, HEADS * HD))
    query_heads, key_heads, value_heads = lax.map(lambda items: head_backward(items[0], items[1], items[2], items[3], pattern), (query_split, key_split, value_split, grad_split))
    return (mixed_out, merge_heads(query_heads), merge_heads(key_heads), merge_heads(value_heads), weight_grad)
```

```python
import math

import jax
import jax.numpy as jnp
from jax import lax
from jax.experimental import pallas as pl
from jax.experimental.pallas import tpu as pltpu
from jax.sharding import Mesh, PartitionSpec as P

HD = 128
BLK = 64


def attend_kernel(pat_ref, q_ref, g_ref, kv_ref, o_ref, dq_ref, dkv_ref, acc_ref):
    X = lax.axis_index("x")
    C = lax.axis_index("c")
    scale = 1.0 / math.sqrt(HD)
    nt = (((1,), (1,)), ((), ()))
    tn = (((0,), (0,)), ((), ()))
    acc_ref[...] = jnp.zeros_like(acc_ref)

    def block(i, carry):
        row = X * 32 + (i // 2) * 4 + C * 2 + i % 2
        offs = []
        for j in range(8):
            p = pat_ref[row, j]
            s = p // 2
            off = ((s % 2) * 4 + s // 16) * 2048 + ((s // 2) % 8) * 128 + (p % 2) * 64
            offs.append(pl.multiple_of(off, 64))
        q = q_ref[pl.ds(pl.multiple_of(i * 64, 64), 64), :]
        g = g_ref[pl.ds(pl.multiple_of(i * 64, 64), 64), :]
        kg = jnp.concatenate([kv_ref[pl.ds(o, 64), :] for o in offs], axis=0)
        vg = jnp.concatenate([kv_ref[pl.ds(o + 1024, 64), :] for o in offs], axis=0)
        s = lax.dot_general(q, kg, nt, preferred_element_type=jnp.float32) * scale
        dp = lax.dot_general(g, vg, nt, preferred_element_type=jnp.float32)
        e = jnp.exp(s - jnp.max(s, axis=-1, keepdims=True))
        p = e / jnp.sum(e, axis=-1, keepdims=True)
        p_low = p.astype(jnp.bfloat16)
        o = jnp.dot(p_low, vg, preferred_element_type=jnp.float32)
        delta = jnp.sum(p * dp, axis=-1, keepdims=True)
        ds = (p * (dp - delta)).astype(jnp.bfloat16)
        dq = jnp.dot(ds, kg, preferred_element_type=jnp.float32) * scale
        dk = lax.dot_general(ds, q, tn, preferred_element_type=jnp.float32) * scale
        dv = lax.dot_general(p_low, g, tn, preferred_element_type=jnp.float32)
        o_ref[pl.ds(pl.multiple_of(i * 64, 64), 64), :] = o.astype(jnp.bfloat16)
        dq_ref[pl.ds(pl.multiple_of(i * 64, 64), 64), :] = dq.astype(jnp.bfloat16)
        for j in range(8):
            acc_ref[pl.ds(offs[j], 64), :] += dk[j * 64 : j * 64 + 64]
            acc_ref[pl.ds(offs[j] + 1024, 64), :] += dv[j * 64 : j * 64 + 64]
        return carry

    lax.fori_loop(0, 16, block, 0)
    dkv_ref[...] = acc_ref[...].astype(jnp.bfloat16)


def attend(pattern, q, g, kv):
    vmem = pl.BlockSpec(memory_space=pltpu.VMEM)
    return pl.pallas_call(
        attend_kernel,
        out_shape=(
            jax.ShapeDtypeStruct((1024, HD), jnp.bfloat16),
            jax.ShapeDtypeStruct((1024, HD), jnp.bfloat16),
            jax.ShapeDtypeStruct((16384, HD), jnp.bfloat16),
        ),
        in_specs=[pl.BlockSpec(memory_space=pltpu.SMEM), vmem, vmem, vmem],
        out_specs=(vmem, vmem, vmem),
        scratch_shapes=[pltpu.VMEM((16384, HD), jnp.float32)],
        compiler_params=pltpu.CompilerParams(vmem_limit_bytes=40 << 20),
        name="attend",
    )(pattern, q, g, kv)


BF = jnp.bfloat16
F32 = jnp.float32
DISTANCES = (1, 7, 2, 6, 3, 5, 4)


def ring(value, step, size):
    return lax.rem(value + step + size, size)


def remote(src, dst, send, recv, **where):
    copy = pltpu.make_async_remote_copy(
        src_ref=src,
        dst_ref=dst,
        send_sem=send,
        recv_sem=recv,
        device_id=where,
        device_id_type=pl.DeviceIdType.MESH,
    )
    copy.start()
    return copy


def greet(peers):
    barrier = pltpu.get_barrier_semaphore()
    for where in peers:
        pl.semaphore_signal(
            barrier, inc=1, device_id=where, device_id_type=pl.DeviceIdType.MESH
        )
    pl.semaphore_wait(barrier, len(peers))


def cols(index, width=128):
    return pl.ds(pl.multiple_of(index * width, width), width)


def dispatch_kernel(
    q_ref, k_ref, v_ref, grad_hbm, weight_hbm,
    kv_ref, qo_ref, go_ref,
    grad, weight, ag,
    in_sem, own_sem, zs, zr, xs, xr, cs, cr,
):
    X, Z, C = (lax.axis_index(n) for n in "xzc")
    load_w = pltpu.make_async_copy(weight_hbm, weight, in_sem.at[0])
    load_g = pltpu.make_async_copy(grad_hbm, grad, in_sem.at[1])
    load_w.start()
    load_g.start()
    right, left, other = ring(X, 1, 4), ring(X, -1, 4), 1 - C
    greet(
        [{"z": ring(Z, d, 8)} for d in DISTANCES] + [{"x": right}, {"x": left}, {"c": other}]
    )

    targets = (
        lambda z: kv_ref.at[C, X, 0, z],
        lambda z: kv_ref.at[C, X, 1, z],
        lambda z: qo_ref.at[z],
        lambda z: go_ref.at[z],
    )

    def spread(t, src):
        sent = [
            remote(
                src.at[:, cols(ring(Z, d, 8))], targets[t](Z), zs.at[t, d], zr.at[t, d],
                z=ring(Z, d, 8),
            )
            for d in DISTANCES
        ]
        own = pltpu.make_async_copy(src.at[:, cols(Z)], targets[t](Z), own_sem.at[t])
        own.start()
        return sent, own

    moved = [spread(0, k_ref), spread(1, v_ref), spread(2, q_ref)]
    load_w.wait()
    load_g.wait()
    ag[...] = lax.dot_general(
        grad[...], weight[...], (((1,), (1,)), ((), ())), preferred_element_type=F32
    ).astype(BF)
    moved.append(spread(3, ag))

    def arrived(t):
        sent, own = moved[t]
        own.wait()
        for copy in sent:
            copy.wait_recv()

    sends = []
    to_right, to_left, to_core = [], [], []
    for t in range(2):
        arrived(t)
        piece = kv_ref.at[C, X, t]
        to_right.append(remote(piece, piece, xs.at[t, 0], xr.at[t, 0], x=right))
        to_left.append(remote(piece, piece, xs.at[t, 1], xr.at[t, 1], x=left))
        to_core.append(remote(piece, piece, cs.at[t, 0], cr.at[t, 0], c=other))
    relay_right, relay_left = [], []
    for t in range(2):
        to_right[t].wait_recv()
        half = kv_ref.at[C, left, t, pl.ds(0, 4)]
        relay_right.append(remote(half, half, xs.at[t, 2], xr.at[t, 2], x=right))
        piece = kv_ref.at[C, left, t]
        to_core.append(remote(piece, piece, cs.at[t, 1], cr.at[t, 1], c=other))
        to_left[t].wait_recv()
        half = kv_ref.at[C, right, t, pl.ds(4, 4)]
        relay_left.append(remote(half, half, xs.at[t, 3], xr.at[t, 3], x=left))
        piece = kv_ref.at[C, right, t]
        to_core.append(remote(piece, piece, cs.at[t, 2], cr.at[t, 2], c=other))
    for t in range(2):
        relay_right[t].wait_recv()
        relay_left[t].wait_recv()
        piece = kv_ref.at[C, ring(X, 2, 4), t]
        to_core.append(remote(piece, piece, cs.at[t, 3], cr.at[t, 3], c=other))
    arrived(2)
    arrived(3)
    for copy in to_core:
        copy.wait_recv()
    for sent, own in moved:
        sends += sent
    for copy in sends + to_right + to_left + relay_right + relay_left + to_core:
        copy.wait_send()


def dispatch(q, k, v, grad, weight):
    vmem = pl.BlockSpec(memory_space=pltpu.VMEM)
    anywhere = pl.BlockSpec(memory_space=pl.ANY)
    dma = pltpu.SemaphoreType.DMA
    return pl.pallas_call(
        dispatch_kernel,
        out_shape=(
            jax.ShapeDtypeStruct((2, 4, 2, 8, 128, HD), BF),
            jax.ShapeDtypeStruct((8, 128, HD), BF),
            jax.ShapeDtypeStruct((8, 128, HD), BF),
        ),
        in_specs=[vmem, vmem, vmem, anywhere, anywhere],
        out_specs=(vmem, vmem, vmem),
        scratch_shapes=[
            pltpu.VMEM((128, 2048), BF),
            pltpu.VMEM((1024, 2048), BF),
            pltpu.VMEM((128, 1024), BF),
            dma((2,)),
            dma((4,)),
            dma((4, 8)),
            dma((4, 8)),
            dma((2, 4)),
            dma((2, 4)),
            dma((2, 4)),
            dma((2, 4)),
        ],
        compiler_params=pltpu.CompilerParams(
            collective_id=0, has_side_effects=True, vmem_limit_bytes=40 << 20
        ),
        name="dispatch",
    )(q, k, v, grad, weight)


def add_slabs(dst, first, *more):
    @pl.loop(0, dst.shape[0])
    def _(i):
        total = first[i].astype(F32)
        for ref in more:
            total += ref[i].astype(F32)
        dst[i] = total.astype(dst.dtype)


def combine_kernel(
    o_ref, dq_ref, dkv_ref, grad, weight_hbm,
    mixed_ref, dqo_ref, dko_ref, dvo_ref, wout_ref,
    weight, att, r, a, xin, xrel, fin, wg, wr, yrel, yin, b, xb, c1, zb, wf,
    in_sem, own_sem, zs, zr, ks, kr, xs, xr, ws, wrs, ys, yr, bs, br, vs, vr, us, ur,
):
    X, Z, C, Y = (lax.axis_index(n) for n in ("x", "z", "c", "rep"))
    load_w = pltpu.make_async_copy(weight_hbm, weight, in_sem.at[0])
    load_w.start()
    right, left, across, other = ring(X, 1, 4), ring(X, -1, 4), ring(X, 2, 4), 1 - C
    up, down, far = ring(Y, 1, 4), ring(Y, -1, 4), ring(Y, 2, 4)
    greet(
        [{"z": ring(Z, d, 8)} for d in DISTANCES]
        + [{"x": right}, {"x": left}, {"x": across}, {"c": other}]
        + [{"rep": up}, {"rep": down}, {"rep": far}]
    )

    def give(t, src, dst):
        sent = [
            remote(src.at[ring(Z, d, 8)], dst.at[:, cols(Z)], zs.at[t, d], zr.at[t, d],
                   z=ring(Z, d, 8))
            for d in DISTANCES
        ]
        own = pltpu.make_async_copy(src.at[Z], dst.at[:, cols(Z)], own_sem.at[t])
        own.start()
        return sent, own

    def arrived(moved):
        moved[1].wait()
        for copy in moved[0]:
            copy.wait_recv()

    sends = []
    att_moved = give(0, o_ref, att)
    chunk_order = (across, right, left, X)
    halves = [
        remote(dkv_ref.at[other, x], r.at[x], ks.at[n], kr.at[n], c=other)
        for n, x in enumerate(chunk_order)
    ]
    sends += halves
    dq_moved = give(1, dq_ref, dqo_ref)

    arrived(att_moved)

    @pl.loop(0, 8)
    def _(h):
        rows = lax.dot_general(
            att[:, cols(h)], grad[...], (((0,), (0,)), ((), ())), preferred_element_type=F32
        ).astype(BF)
        for n in range(8):
            for y in range(4):
                wg[n % 2, y, h * 4 + n // 2] = rows[n * 16 : n * 16 + 16, y * 512 : y * 512 + 512]

    y_order = (far, up, down, Y)
    w_halves = [
        remote(wg.at[other, y], wr.at[y], ws.at[n], wrs.at[n], c=other)
        for n, y in enumerate(y_order)
    ]
    sends += w_halves

    def add_piece(dst, *more):
        for t in range(2):
            add_slabs(dst.at[t], *[ref.at[t] for ref in more])

    halves[0].wait_recv()
    add_piece(a.at[across], dkv_ref.at[C, across], r.at[across])
    relay_a = remote(a.at[across, 0], xrel.at[0], xs.at[0], xr.at[0], x=right)
    relay_b = remote(a.at[across, 1], xrel.at[1], xs.at[1], xr.at[1], x=left)
    halves[1].wait_recv()
    add_piece(a.at[right], dkv_ref.at[C, right], r.at[right])
    near_a = remote(a.at[right, 1], xin.at[0, 1], xs.at[2], xr.at[2], x=right)
    halves[2].wait_recv()
    add_piece(a.at[left], dkv_ref.at[C, left], r.at[left])
    near_b = remote(a.at[left, 0], xin.at[1, 0], xs.at[3], xr.at[3], x=left)

    w_halves[0].wait_recv()
    add_slabs(wr.at[far], wg.at[C, far], wr.at[far])
    yrelay_a = remote(
        wr.at[far, pl.ds(0, 16)], yrel.at[0], ys.at[0], yr.at[0], rep=up
    )
    yrelay_b = remote(
        wr.at[far, pl.ds(16, 16)], yrel.at[1], ys.at[1], yr.at[1], rep=down
    )
    w_halves[1].wait_recv()
    add_slabs(wr.at[up], wg.at[C, up], wr.at[up])
    ynear_a = remote(
        wr.at[up, pl.ds(16, 16)], yin.at[0, pl.ds(16, 16)], ys.at[2], yr.at[2], rep=up
    )
    w_halves[2].wait_recv()
    add_slabs(wr.at[down], wg.at[C, down], wr.at[down])
    ynear_b = remote(
        wr.at[down, pl.ds(0, 16)], yin.at[1, pl.ds(0, 16)], ys.at[3], yr.at[3], rep=down
    )

    relay_a.wait_recv()
    add_slabs(xrel.at[0], a.at[right, 0], xrel.at[0])
    last_a = remote(xrel.at[0], xin.at[0, 0], xs.at[4], xr.at[4], x=right)
    relay_b.wait_recv()
    add_slabs(xrel.at[1], a.at[left, 1], xrel.at[1])
    last_b = remote(xrel.at[1], xin.at[1, 1], xs.at[5], xr.at[5], x=left)

    halves[3].wait_recv()
    add_piece(a.at[X], dkv_ref.at[C, X], r.at[X])

    yrelay_a.wait_recv()
    add_slabs(yrel.at[0], wr.at[up, pl.ds(0, 16)], yrel.at[0])
    ylast_a = remote(yrel.at[0], yin.at[0, pl.ds(0, 16)], ys.at[4], yr.at[4], rep=up)
    yrelay_b.wait_recv()
    add_slabs(yrel.at[1], wr.at[down, pl.ds(16, 16)], yrel.at[1])
    ylast_b = remote(yrel.at[1], yin.at[1, pl.ds(16, 16)], ys.at[5], yr.at[5], rep=down)
    w_halves[3].wait_recv()
    add_slabs(wr.at[Y], wg.at[C, Y], wr.at[Y])

    load_w.wait()
    mixed_ref[...] = jnp.dot(att[...], weight[...], preferred_element_type=F32).astype(BF)

    near_b.wait_recv()
    last_a.wait_recv()
    add_slabs(fin.at[0], a.at[X, 0], xin.at[0, 0], xin.at[1, 0])
    dk_moved = give(2, fin.at[0], dko_ref)
    near_a.wait_recv()
    last_b.wait_recv()
    add_slabs(fin.at[1], a.at[X, 1], xin.at[0, 1], xin.at[1, 1])
    dv_moved = give(3, fin.at[1], dvo_ref)

    for copy in (ynear_a, ynear_b, ylast_a, ylast_b):
        copy.wait_recv()
    add_slabs(b, wr.at[Y], yin.at[0], yin.at[1])

    def slabs(x):
        return b.at[pl.ds(pl.multiple_of(x * 8, 8), 8)]

    b_moved = [
        remote(slabs(ring(X, d, 4)), xb.at[d], bs.at[d], br.at[d], x=ring(X, d, 4))
        for d in (1, 3, 2)
    ]
    for copy in b_moved:
        copy.wait_recv()
    add_slabs(c1, slabs(X), xb.at[1], xb.at[2], xb.at[3])
    c_moved = [
        remote(c1.at[ring(Z, d, 8)], zb.at[d], vs.at[d], vr.at[d], z=ring(Z, d, 8))
        for d in DISTANCES
    ]
    for copy in c_moved:
        copy.wait_recv()
    total = c1[Z].astype(F32)
    for d in DISTANCES:
        total += zb[d].astype(F32)
    total = total * (1.0 / math.sqrt(32768))
    wf[...] = total
    wout_ref[:, cols(Y, 512)] = total
    u_moved = [
        remote(wf, wout_ref.at[:, cols(Y, 512)], us.at[d], ur.at[d], rep=ring(Y, d, 4))
        for d in (1, 3, 2)
    ]
    arrived(dq_moved)
    arrived(dk_moved)
    arrived(dv_moved)
    for copy in u_moved:
        copy.wait_recv()
    for moved in (att_moved, dq_moved, dk_moved, dv_moved):
        sends += moved[0]
    sends += [relay_a, relay_b, near_a, near_b, last_a, last_b]
    sends += [yrelay_a, yrelay_b, ynear_a, ynear_b, ylast_a, ylast_b]
    for copy in sends + b_moved + c_moved + u_moved:
        copy.wait_send()


def combine(o, dq, dkv, grad, weight):
    vmem = pl.BlockSpec(memory_space=pltpu.VMEM)
    anywhere = pl.BlockSpec(memory_space=pl.ANY)
    dma = pltpu.SemaphoreType.DMA
    return pl.pallas_call(
        combine_kernel,
        out_shape=(
            jax.ShapeDtypeStruct((128, 2048), BF),
            jax.ShapeDtypeStruct((128, 1024), BF),
            jax.ShapeDtypeStruct((128, 1024), BF),
            jax.ShapeDtypeStruct((128, 1024), BF),
            jax.ShapeDtypeStruct((16, 2048), F32),
        ),
        in_specs=[vmem, vmem, vmem, vmem, anywhere],
        out_specs=(vmem,) * 5,
        scratch_shapes=[
            pltpu.VMEM((1024, 2048), BF),
            pltpu.VMEM((128, 1024), BF),
            pltpu.VMEM((4, 2, 8, 128, HD), BF),
            pltpu.VMEM((4, 2, 8, 128, HD), BF),
            pltpu.VMEM((2, 2, 8, 128, HD), BF),
            pltpu.VMEM((2, 8, 128, HD), BF),
            pltpu.VMEM((2, 8, 128, HD), BF),
            pltpu.VMEM((2, 4, 32, 16, 512), BF),
            pltpu.VMEM((4, 32, 16, 512), BF),
            pltpu.VMEM((2, 16, 16, 512), BF),
            pltpu.VMEM((2, 32, 16, 512), BF),
            pltpu.VMEM((32, 16, 512), BF),
            pltpu.VMEM((4, 8, 16, 512), BF),
            pltpu.VMEM((8, 16, 512), BF),
            pltpu.VMEM((8, 16, 512), BF),
            pltpu.VMEM((16, 512), F32),
            dma((1,)),
            dma((4,)),
            dma((4, 8)),
            dma((4, 8)),
            dma((4,)),
            dma((4,)),
            dma((6,)),
            dma((6,)),
            dma((4,)),
            dma((4,)),
            dma((6,)),
            dma((6,)),
            dma((4,)),
            dma((4,)),
            dma((8,)),
            dma((8,)),
            dma((4,)),
            dma((4,)),
        ],
        compiler_params=pltpu.CompilerParams(
            collective_id=1, has_side_effects=True, vmem_limit_bytes=56 << 20
        ),
        name="combine",
    )(o, dq, dkv, grad, weight)


def local(query_in, key_in, value_in, out_weight, grad_out, pattern):
    kv, q, g = dispatch(query_in[0], key_in[0], value_in[0], grad_out[0], out_weight)
    o, dq, dkv = attend(
        pattern, q.reshape(1024, HD), g.reshape(1024, HD), kv.reshape(16384, HD)
    )
    mixed_out, query_grad, key_grad, value_grad, weight_grad = combine(
        o.reshape(8, 128, HD), dq.reshape(8, 128, HD), dkv.reshape(2, 4, 2, 8, 128, HD),
        grad_out[0], out_weight,
    )
    return (mixed_out[None], query_grad[None], key_grad[None], value_grad[None], weight_grad)


def solution(mesh):
    devices = mesh.devices.reshape(4, 8, 2, 4)
    inner = Mesh(devices, ("x", "z", "c", "rep"))
    seq = ("x", "z", "c")
    rows = P("rep", seq, None)
    return jax.shard_map(
        local,
        mesh=inner,
        in_specs=(rows, rows, rows, P(), rows, P()),
        out_specs=(rows, rows, rows, rows, P(seq, None)),
        check_vma=False,
    )
```

```python
import math

import jax
import jax.numpy as jnp
from jax import lax
from jax.experimental import pallas as pl
from jax.experimental.pallas import tpu as pltpu
from jax.sharding import Mesh, PartitionSpec as P

HD = 128
BLK = 64
BF = jnp.bfloat16
F32 = jnp.float32
SCALE = 1.0 / math.sqrt(HD)
DISTANCES = (1, 7, 2, 6, 3, 5, 4)
NT = (((1,), (1,)), ((), ()))
TN = (((0,), (0,)), ((), ()))


def ring(value, step, size):
    return lax.rem(value + step + size, size)


def link(src, dst, send, recv, **where):
    return pltpu.make_async_remote_copy(
        src_ref=src,
        dst_ref=dst,
        send_sem=send,
        recv_sem=recv,
        device_id=where,
        device_id_type=pl.DeviceIdType.MESH,
    )


def remote(src, dst, send, recv, **where):
    copy = link(src, dst, send, recv, **where)
    copy.start()
    return copy


def greet(peers):
    barrier = pltpu.get_barrier_semaphore()
    for where in peers:
        pl.semaphore_signal(
            barrier, inc=1, device_id=where, device_id_type=pl.DeviceIdType.MESH
        )
    pl.semaphore_wait(barrier, len(peers))


def span(index, width):
    return pl.ds(pl.multiple_of(index * width, width), width)


def cols(index, width=128):
    return span(index, width)


def add_slabs(dst, first, *more):
    @pl.loop(0, dst.shape[0])
    def _(i):
        total = first[i].astype(F32)
        for ref in more:
            total += ref[i].astype(F32)
        dst[i] = total.astype(dst.dtype)


def layer_kernel(
    tbl, q_hbm, k_hbm, v_hbm, grad_hbm, weight_hbm,
    mixed_hbm, dqo_ref, dko_ref, dvo_ref, wout_ref,
    q_in, k_in, v_in, grad, weight, ag, kv, qs, gs, probs, o, dq, att, segk, segv,
    given, r, a, xin, xrel, fin, wg, wr, yrel, yin, b, xb, c1, zb, wf, mixed,
    in_sem, own_sem, zs, zr, fs, fr, ks, kr, xs, xr, ws, wrs, ys, yr, bs, br, vs, vr, us, ur,
):
    X, Z, C, Y = (lax.axis_index(n) for n in ("x", "z", "c", "rep"))
    loads = [
        pltpu.make_async_copy(src, dst, in_sem.at[n])
        for n, (src, dst) in enumerate(
            ((k_hbm, k_in), (v_hbm, v_in), (q_hbm, q_in), (grad_hbm, grad), (weight_hbm, weight))
        )
    ]
    for copy in loads:
        copy.start()
    right, left, across, other = ring(X, 1, 4), ring(X, -1, 4), ring(X, 2, 4), 1 - C
    up, down, far = ring(Y, 1, 4), ring(Y, -1, 4), ring(Y, 2, 4)
    greet(
        [{"z": ring(Z, d, 8)} for d in DISTANCES]
        + [{"x": right}, {"x": left}, {"x": across}, {"c": other}]
        + [{"rep": up}, {"rep": down}, {"rep": far}]
    )

    def piece(c, x, t, first=0, count=8):
        return kv.at[pl.ds((((c * 4 + x) * 2 + t) * 8 + first) * 2, count * 2)]

    targets = (
        lambda: piece(C, X, 0, Z, 1),
        lambda: piece(C, X, 1, Z, 1),
        lambda: qs.at[pl.ds(Z * 2, 2)],
        lambda: gs.at[pl.ds(Z * 2, 2)],
    )

    def spread(t, src):
        sent = [
            remote(
                src.at[:, :, cols(ring(Z, d, 8))], targets[t](), zs.at[t, d], zr.at[t, d],
                z=ring(Z, d, 8),
            )
            for d in DISTANCES
        ]
        own = pltpu.make_async_copy(src.at[:, :, cols(Z)], targets[t](), own_sem.at[t])
        own.start()
        return sent, own

    def arrived(moved):
        moved[1].wait()
        for copy in moved[0]:
            copy.wait_recv()

    loads[0].wait()
    k_moved = spread(0, k_in)
    loads[1].wait()
    v_moved = spread(1, v_in)
    loads[2].wait()
    q_moved = spread(2, q_in)
    segk[128] = jnp.zeros((BLK, HD), F32)
    segv[128] = jnp.zeros((BLK, HD), F32)
    loads[3].wait()
    loads[4].wait()
    rows = lax.dot_general(grad[...], weight[...], NT, preferred_element_type=F32).astype(BF)
    ag[0] = rows[:64]
    ag[1] = rows[64:]
    g_moved = spread(3, ag)

    to_right, to_left, to_core = [], [], []
    for t, moved in enumerate((k_moved, v_moved)):
        arrived(moved)
        here = piece(C, X, t)
        to_right.append(remote(here, here, fs.at[t, 0], fr.at[t, 0], x=right))
        to_left.append(remote(here, here, fs.at[t, 1], fr.at[t, 1], x=left))
        to_core.append(remote(here, here, fs.at[t, 2], fr.at[t, 2], c=other))
    relays = []
    for t in range(2):
        to_right[t].wait_recv()
        half = piece(C, left, t, 0, 4)
        relays.append(remote(half, half, fs.at[t, 3], fr.at[t, 3], x=right))
        here = piece(C, left, t)
        to_core.append(remote(here, here, fs.at[t, 4], fr.at[t, 4], c=other))
        to_left[t].wait_recv()
        half = piece(C, right, t, 4, 4)
        relays.append(remote(half, half, fs.at[t, 5], fr.at[t, 5], x=left))
        here = piece(C, right, t)
        to_core.append(remote(here, here, fs.at[t, 6], fr.at[t, 6], c=other))
    for t in range(2):
        relays[2 * t].wait_recv()
        relays[2 * t + 1].wait_recv()
        here = piece(C, across, t)
        to_core.append(remote(here, here, fs.at[t, 7], fr.at[t, 7], c=other))
    arrived(q_moved)
    for copy in to_core:
        copy.wait_recv()

    def gathered(i, extra):
        return jnp.concatenate(
            [
                kv[tbl[0, i * 8 + j] + extra]
                for j in range(8)
            ],
            axis=0,
        )

    def out_copy(t, n, src, dst):
        z = lax.rem(Z + n + 1, 8)
        return link(
            src.at[span(z, 128)], dst.at[:, cols(Z)], zs.at[t, n + 1], zr.at[t, n + 1], z=z
        )

    @pl.loop(0, 8)
    def _(n):
        z = lax.rem(Z + n + 1, 8)
        for half in range(2):
            i = z * 2 + half
            rows = span(i, 64)
            s = lax.dot_general(qs[i], gathered(i, 0), NT, preferred_element_type=F32) * SCALE
            e = jnp.exp(s - jnp.max(s, axis=-1, keepdims=True))
            p = e / jnp.sum(e, axis=-1, keepdims=True)
            probs[rows, :] = p
            o[rows, :] = jnp.dot(
                p.astype(BF), gathered(i, 16), preferred_element_type=F32
            ).astype(BF)

        @pl.when(n < 7)
        def _():
            out_copy(4, n, o, att).start()

    att_own = pltpu.make_async_copy(o.at[span(Z, 128)], att.at[:, cols(Z)], own_sem.at[4])
    att_own.start()
    att_moved = [out_copy(4, n, o, att) for n in range(7)], att_own
    arrived(g_moved)

    def backward(first, last):
        @pl.loop(first, last)
        def _(n):
            z = lax.rem(Z + n + 1, 8)
            for half in range(2):
                i = z * 2 + half
                rows = span(i, 64)
                q, g, p = qs[i], gs[i], probs[rows, :]
                kg = gathered(i, 0)
                dp = lax.dot_general(g, gathered(i, 16), NT, preferred_element_type=F32)
                delta = jnp.sum(p * dp, axis=-1, keepdims=True)
                ds = (p * (dp - delta)).astype(BF)
                dq[rows, :] = (
                    jnp.dot(ds, kg, preferred_element_type=F32) * SCALE
                ).astype(BF)
                dk = lax.dot_general(ds, q, TN, preferred_element_type=F32)
                dv = lax.dot_general(p.astype(BF), g, TN, preferred_element_type=F32)
                m = n * 2 + half
                for j in range(8):
                    before = tbl[1, m * 8 + j]
                    segk[m * 8 + j] = segk[before] + dk[j * 64 : j * 64 + 64]
                    segv[m * 8 + j] = segv[before] + dv[j * 64 : j * 64 + 64]

            @pl.when(n < 7)
            def _():
                out_copy(5, n, dq, dqo_ref).start()

    backward(0, 4)
    arrived(att_moved)

    @pl.loop(0, 8)
    def _(h):
        rows = lax.dot_general(att[:, cols(h)], grad[...], TN, preferred_element_type=F32).astype(BF)
        for n in range(8):
            for y in range(4):
                wg[n % 2, y, h * 4 + n // 2] = rows[n * 16 : n * 16 + 16, y * 512 : y * 512 + 512]

    w_halves = [
        remote(wg.at[other, y], wr.at[y], ws.at[n], wrs.at[n], c=other)
        for n, y in enumerate((far, up, down, Y))
    ]
    backward(4, 6)

    low, high = pl.ds(0, 16), pl.ds(16, 16)
    w_halves[0].wait_recv()
    add_slabs(wr.at[far], wg.at[C, far], wr.at[far])
    yrelay_a = remote(wr.at[far, low], yrel.at[0], ys.at[0], yr.at[0], rep=up)
    yrelay_b = remote(wr.at[far, high], yrel.at[1], ys.at[1], yr.at[1], rep=down)
    w_halves[1].wait_recv()
    add_slabs(wr.at[up], wg.at[C, up], wr.at[up])
    ynear_a = remote(wr.at[up, high], yin.at[0, high], ys.at[2], yr.at[2], rep=up)
    w_halves[2].wait_recv()
    add_slabs(wr.at[down], wg.at[C, down], wr.at[down])
    ynear_b = remote(wr.at[down, low], yin.at[1, low], ys.at[3], yr.at[3], rep=down)
    w_halves[3].wait_recv()
    add_slabs(wr.at[Y], wg.at[C, Y], wr.at[Y])

    backward(6, 8)
    dq_own = pltpu.make_async_copy(dq.at[span(Z, 128)], dqo_ref.at[:, cols(Z)], own_sem.at[5])
    dq_own.start()
    dq_moved = [out_copy(5, n, dq, dqo_ref) for n in range(7)], dq_own

    def collect(x, core, dst, more=None):
        @pl.loop(0, 8)
        def _(z):
            for half in range(2):
                slot = tbl[2, x * 32 + z * 4 + core * 2 + half]
                rows = slice(half * 64, half * 64 + 64)
                for t, total in enumerate((segk[slot] * SCALE, segv[slot])):
                    if more is not None:
                        total += more[t, z, rows].astype(F32)
                    dst[t, z, rows] = total.astype(BF)

    halves = []
    for n, x in enumerate((across, right, left, X)):
        collect(x, other, given.at[x])
        halves.append(remote(given.at[x], r.at[x], ks.at[n], kr.at[n], c=other))

    halves[0].wait_recv()
    collect(across, C, a.at[across], r.at[across])
    relay_a = remote(a.at[across, 0], xrel.at[0], xs.at[0], xr.at[0], x=right)
    relay_b = remote(a.at[across, 1], xrel.at[1], xs.at[1], xr.at[1], x=left)
    halves[1].wait_recv()
    collect(right, C, a.at[right], r.at[right])
    near_a = remote(a.at[right, 1], xin.at[0, 1], xs.at[2], xr.at[2], x=right)
    halves[2].wait_recv()
    collect(left, C, a.at[left], r.at[left])
    near_b = remote(a.at[left, 0], xin.at[1, 0], xs.at[3], xr.at[3], x=left)

    yrelay_a.wait_recv()
    add_slabs(yrel.at[0], wr.at[up, low], yrel.at[0])
    ylast_a = remote(yrel.at[0], yin.at[0, low], ys.at[4], yr.at[4], rep=up)
    yrelay_b.wait_recv()
    add_slabs(yrel.at[1], wr.at[down, high], yrel.at[1])
    ylast_b = remote(yrel.at[1], yin.at[1, high], ys.at[5], yr.at[5], rep=down)

    halves[3].wait_recv()
    collect(X, C, a.at[X], r.at[X])
    mixed[...] = jnp.dot(att[...], weight[...], preferred_element_type=F32).astype(BF)
    mixed_out = pltpu.make_async_copy(mixed, mixed_hbm, in_sem.at[5])
    mixed_out.start()

    relay_a.wait_recv()
    add_slabs(xrel.at[0], a.at[right, 0], xrel.at[0])
    last_a = remote(xrel.at[0], xin.at[0, 0], xs.at[4], xr.at[4], x=right)
    relay_b.wait_recv()
    add_slabs(xrel.at[1], a.at[left, 1], xrel.at[1])
    last_b = remote(xrel.at[1], xin.at[1, 1], xs.at[5], xr.at[5], x=left)

    for copy in (ynear_a, ynear_b, ylast_a, ylast_b):
        copy.wait_recv()
    add_slabs(b, wr.at[Y], yin.at[0], yin.at[1])

    def slabs(x):
        return b.at[span(x, 8)]

    b_moved = [
        remote(slabs(ring(X, d, 4)), xb.at[d], bs.at[d], br.at[d], x=ring(X, d, 4))
        for d in (1, 3, 2)
    ]

    def give(t, src, dst):
        sent = [
            remote(src.at[ring(Z, d, 8)], dst.at[:, cols(Z)], zs.at[t, d], zr.at[t, d],
                   z=ring(Z, d, 8))
            for d in DISTANCES
        ]
        own = pltpu.make_async_copy(src.at[Z], dst.at[:, cols(Z)], own_sem.at[t])
        own.start()
        return sent, own

    near_b.wait_recv()
    last_a.wait_recv()
    add_slabs(fin.at[0], a.at[X, 0], xin.at[0, 0], xin.at[1, 0])
    dk_moved = give(6, fin.at[0], dko_ref)
    near_a.wait_recv()
    last_b.wait_recv()
    add_slabs(fin.at[1], a.at[X, 1], xin.at[0, 1], xin.at[1, 1])
    dv_moved = give(7, fin.at[1], dvo_ref)

    for copy in b_moved:
        copy.wait_recv()
    add_slabs(c1, slabs(X), xb.at[1], xb.at[2], xb.at[3])
    c_moved = [
        remote(c1.at[ring(Z, d, 8)], zb.at[d], vs.at[d], vr.at[d], z=ring(Z, d, 8))
        for d in DISTANCES
    ]
    for copy in c_moved:
        copy.wait_recv()
    total = c1[Z].astype(F32)
    for d in DISTANCES:
        total += zb[d].astype(F32)
    wf[...] = total * (1.0 / math.sqrt(32768))
    w_own = pltpu.make_async_copy(wf, wout_ref.at[:, cols(Y, 512)], in_sem.at[6])
    w_own.start()
    u_moved = [
        remote(wf, wout_ref.at[:, cols(Y, 512)], us.at[d], ur.at[d], rep=ring(Y, d, 4))
        for d in (1, 3, 2)
    ]
    arrived(dq_moved)
    arrived(dk_moved)
    arrived(dv_moved)
    for copy in u_moved:
        copy.wait_recv()
    w_own.wait()
    mixed_out.wait()
    sends = []
    for moved in (k_moved, v_moved, q_moved, g_moved, att_moved, dq_moved, dk_moved, dv_moved):
        sends += moved[0]
    sends += to_right + to_left + to_core + relays + w_halves + halves
    sends += [relay_a, relay_b, near_a, near_b, last_a, last_b]
    sends += [yrelay_a, yrelay_b, ynear_a, ynear_b, ylast_a, ylast_b]
    for copy in sends + b_moved + c_moved + u_moved:
        copy.wait_send()


OUTPUTS = (
    jax.ShapeDtypeStruct((128, 2048), BF),
    jax.ShapeDtypeStruct((128, 1024), BF),
    jax.ShapeDtypeStruct((128, 1024), BF),
    jax.ShapeDtypeStruct((128, 1024), BF),
    jax.ShapeDtypeStruct((16, 2048), F32),
)


def layer(tables, q, k, v, grad, weight):
    anywhere = pl.BlockSpec(memory_space=pl.ANY)
    dma = pltpu.SemaphoreType.DMA
    vm = pltpu.VMEM
    return pl.pallas_call(
        layer_kernel,
        out_shape=OUTPUTS,
        in_specs=[pl.BlockSpec(memory_space=pltpu.SMEM)] + [anywhere] * 5,
        out_specs=(anywhere,) * 5,
        scratch_shapes=[
            vm((2, BLK, 1024), BF),
            vm((2, BLK, 1024), BF),
            vm((2, BLK, 1024), BF),
            vm((128, 2048), BF),
            vm((1024, 2048), BF),
            vm((2, BLK, 1024), BF),
            vm((256, BLK, HD), BF),
            vm((16, BLK, HD), BF),
            vm((16, BLK, HD), BF),
            vm((1024, 512), F32),
            vm((1024, HD), BF),
            vm((1024, HD), BF),
            vm((128, 1024), BF),
            vm((129, BLK, HD), F32),
            vm((129, BLK, HD), F32),
            vm((4, 2, 8, 128, HD), BF),
            vm((4, 2, 8, 128, HD), BF),
            vm((4, 2, 8, 128, HD), BF),
            vm((2, 2, 8, 128, HD), BF),
            vm((2, 8, 128, HD), BF),
            vm((2, 8, 128, HD), BF),
            vm((2, 4, 32, 16, 512), BF),
            vm((4, 32, 16, 512), BF),
            vm((2, 16, 16, 512), BF),
            vm((2, 32, 16, 512), BF),
            vm((32, 16, 512), BF),
            vm((4, 8, 16, 512), BF),
            vm((8, 16, 512), BF),
            vm((8, 16, 512), BF),
            vm((16, 512), F32),
            vm((128, 2048), BF),
            dma((7,)),
            dma((8,)),
            dma((8, 8)),
            dma((8, 8)),
            dma((2, 8)),
            dma((2, 8)),
            dma((4,)),
            dma((4,)),
            dma((6,)),
            dma((6,)),
            dma((4,)),
            dma((4,)),
            dma((6,)),
            dma((6,)),
            dma((4,)),
            dma((4,)),
            dma((8,)),
            dma((8,)),
            dma((4,)),
            dma((4,)),
        ],
        compiler_params=pltpu.CompilerParams(
            collective_id=0, has_side_effects=True, vmem_limit_bytes=63 << 20
        ),
        name="layer",
    )(tables, q, k, v, grad, weight)


def finish_kernel(*refs):
    sources, results, held, sems = refs[:5], refs[5:10], refs[10:15], refs[15]
    taken = [
        pltpu.make_async_copy(src, buf, sems.at[n])
        for n, (src, buf) in enumerate(zip(sources, held))
    ]
    put = [
        pltpu.make_async_copy(buf, dst, sems.at[5 + n])
        for n, (buf, dst) in enumerate(zip(held, results))
    ]
    for copy in taken:
        copy.start()
    for copy, onward in zip(taken, put):
        copy.wait()
        onward.start()
    for copy in put:
        copy.wait()


def finish(arrays):
    anywhere = pl.BlockSpec(memory_space=pl.ANY)
    return pl.pallas_call(
        finish_kernel,
        out_shape=OUTPUTS,
        in_specs=[anywhere] * 5,
        out_specs=(anywhere,) * 5,
        scratch_shapes=[pltpu.VMEM(s.shape, s.dtype) for s in OUTPUTS]
        + [pltpu.SemaphoreType.DMA((10,))],
        compiler_params=pltpu.CompilerParams(vmem_limit_bytes=63 << 20),
        name="finish",
    )(*arrays)


def tables_of(pattern):
    X, Z, C = (lax.axis_index(n) for n in "xzc")
    by_owner = pattern.reshape(4, 8, 2, 16)
    mine = lax.dynamic_slice(by_owner, (X, 0, C, 0), (1, 8, 1, 16)).reshape(8, 16)
    plain = mine.reshape(128)
    turned = jnp.concatenate([mine, mine], axis=0)
    turned = lax.dynamic_slice(turned, (lax.rem(Z + 1, 8), 0), (8, 16)).reshape(128)
    s = plain // 2
    places = ((s % 2) * 4 + s // 16) * 32 + ((s // 2) % 8) * 2 + plain % 2
    order = jnp.arange(128, dtype=jnp.int32)
    same = turned[None, :] == turned[:, None]
    earlier = order[None, :] < order[:, None]
    before = jnp.max(jnp.where(same & earlier, order[None, :], -1), axis=1)
    last = jnp.max(jnp.where(turned[None, :] == order[:, None], order[None, :], -1), axis=1)
    return jnp.stack(
        [places, jnp.where(before < 0, 128, before), jnp.where(last < 0, 128, last)]
    )


def local(query_in, key_in, value_in, out_weight, grad_out, pattern):
    results = layer(
        tables_of(pattern),
        *(a.reshape(2, BLK, 1024) for a in (query_in, key_in, value_in)),
        grad_out[0],
        out_weight,
    )
    mixed_out, query_grad, key_grad, value_grad, weight_grad = finish(results)
    return (mixed_out[None], query_grad[None], key_grad[None], value_grad[None], weight_grad)


def solution(mesh):
    devices = mesh.devices.reshape(4, 8, 2, 4)
    inner = Mesh(devices, ("x", "z", "c", "rep"))
    seq = ("x", "z", "c")
    rows = P("rep", seq, None)
    return jax.shard_map(
        local,
        mesh=inner,
        in_specs=(rows, rows, rows, P(), rows, P()),
        out_specs=(rows, rows, rows, rows, P(seq, None)),
        check_vma=False,
    )
```

```python
import math

import jax
import jax.numpy as jnp
from jax import lax
from jax.experimental import pallas as pl
from jax.experimental.pallas import tpu as pltpu
from jax.sharding import Mesh, PartitionSpec as P

HD = 128
BLK = 64
BF = jnp.bfloat16
F32 = jnp.float32
SCALE = 1.0 / math.sqrt(HD)
DISTANCES = (1, 7, 2, 6, 3, 5, 4)
ARRIVALS = (0,) + DISTANCES
NT = (((1,), (1,)), ((), ()))
TN = (((0,), (0,)), ((), ()))


def ring(value, step, size):
    return lax.rem(value + step + size, size)


def link(src, dst, send, recv, **where):
    return pltpu.make_async_remote_copy(
        src_ref=src,
        dst_ref=dst,
        send_sem=send,
        recv_sem=recv,
        device_id=where,
        device_id_type=pl.DeviceIdType.MESH,
    )


def remote(src, dst, send, recv, **where):
    copy = link(src, dst, send, recv, **where)
    copy.start()
    return copy


def greet(peers):
    barrier = pltpu.get_barrier_semaphore()
    for where in peers:
        pl.semaphore_signal(
            barrier, inc=1, device_id=where, device_id_type=pl.DeviceIdType.MESH
        )
    pl.semaphore_wait(barrier, len(peers))


def span(index, width):
    return pl.ds(pl.multiple_of(index * width, width), width)


def cols(index, width=128):
    return span(index, width)


def add_slabs(dst, first, *more):
    @pl.loop(0, dst.shape[0])
    def _(i):
        total = first[i].astype(F32)
        for ref in more:
            total += ref[i].astype(F32)
        dst[i] = total.astype(dst.dtype)


def layer_kernel(
    tbl, q_hbm, k_hbm, v_hbm, grad_hbm, weight_hbm,
    mixed_hbm, dqo_ref, dko_ref, dvo_ref, wout_ref,
    q_in, k_in, v_in, grad, weight, ag, kv, qs, gs, probs, o, dq, att, segk, segv,
    given, r, a, xin, xrel, fin, wg, wr, yrel, yin, b, xb, c1, zb, wf, mixed, turned,
    in_sem, own_sem, zs, zr, fs, fr, cs, cr, ks, kr, xs, xr, ws, wrs, ys, yr, bs, br, vs, vr, us, ur,
):
    X, Z, C, Y = (lax.axis_index(n) for n in ("x", "z", "c", "rep"))
    loads = [
        pltpu.make_async_copy(src, dst, in_sem.at[n])
        for n, (src, dst) in enumerate(
            ((k_hbm, k_in), (v_hbm, v_in), (q_hbm, q_in), (grad_hbm, grad), (weight_hbm, weight))
        )
    ]
    for copy in loads:
        copy.start()
    right, left, across, other = ring(X, 1, 4), ring(X, -1, 4), ring(X, 2, 4), 1 - C
    up, down, far = ring(Y, 1, 4), ring(Y, -1, 4), ring(Y, 2, 4)
    greet(
        [{"z": ring(Z, d, 8)} for d in DISTANCES]
        + [{"x": right}, {"x": left}, {"x": across}, {"c": other}]
        + [{"rep": up}, {"rep": down}, {"rep": far}]
    )

    def piece(c, x, t, first=0, count=8):
        return kv.at[pl.ds((((c * 4 + x) * 2 + t) * 8 + first) * 2, count * 2)]

    targets = (
        lambda: piece(C, X, 0, Z, 1),
        lambda: piece(C, X, 1, Z, 1),
        lambda: qs.at[pl.ds(Z * 2, 2)],
        lambda: gs.at[pl.ds(Z * 2, 2)],
    )

    def spread(t, src):
        sent = [
            remote(
                src.at[:, :, cols(ring(Z, d, 8))], targets[t](), zs.at[t, d], zr.at[t, d],
                z=ring(Z, d, 8),
            )
            for d in DISTANCES
        ]
        own = pltpu.make_async_copy(src.at[:, :, cols(Z)], targets[t](), own_sem.at[t])
        own.start()
        return sent, own

    def arrived(moved):
        moved[1].wait()
        for copy in moved[0]:
            copy.wait_recv()

    loads[0].wait()
    k_moved = spread(0, k_in)
    loads[1].wait()
    v_moved = spread(1, v_in)
    loads[2].wait()
    q_moved = spread(2, q_in)
    segk[128] = jnp.zeros((BLK, HD), F32)
    segv[128] = jnp.zeros((BLK, HD), F32)
    loads[3].wait()
    loads[4].wait()
    rows = lax.dot_general(grad[...], weight[...], NT, preferred_element_type=F32).astype(BF)
    ag[0] = rows[:64]
    ag[1] = rows[64:]
    g_moved = spread(3, ag)

    near, relays, to_core = {}, {}, []

    def send_near(t, d):
        if d == 0:
            moves[t][1].wait()
        else:
            moves[t][0][DISTANCES.index(d)].wait_recv()
        here = piece(C, X, t, ring(Z, -d, 8), 1)
        near[t, d] = (
            remote(here, here, fs.at[t, d, 0], fr.at[t, d, 0], x=right),
            remote(here, here, fs.at[t, d, 1], fr.at[t, d, 1], x=left),
        )

    def send_relay(t, d):
        for copy in near[t, d]:
            copy.wait_recv()
        source, target = (left, right) if d < 4 else (right, left)
        here = piece(C, source, t, ring(Z, -d, 8), 1)
        relays[t, d] = remote(here, here, fs.at[t, d, 2], fr.at[t, d, 2], x=target)

    def across_core(t, n, x):
        here = piece(C, x, t)
        to_core.append(remote(here, here, cs.at[t, n], cr.at[t, n], c=other))

    moves = (k_moved, v_moved)
    steps = [(t, d) for t in range(2) for d in ARRIVALS]
    for n in range(len(steps) + 4):
        if n < len(steps):
            send_near(*steps[n])
            if n % 8 == 7:
                across_core(n // 8, 0, X)
        if n >= 4:
            send_relay(*steps[n - 4])
            if n % 8 == 3:
                across_core(n // 8 - 1, 1, left)
                across_core(n // 8 - 1, 2, right)
    for t in range(2):
        for d in ARRIVALS:
            relays[t, d].wait_recv()
            here = piece(C, across, t, ring(Z, -d, 8), 1)
            to_core.append(remote(here, here, cs.at[t, 3 + d], cr.at[t, 3 + d], c=other))
    arrived(q_moved)
    for copy in to_core:
        copy.wait_recv()

    def gathered(i, extra):
        return jnp.concatenate(
            [
                kv[tbl[0, i * 8 + j] + extra]
                for j in range(8)
            ],
            axis=0,
        )

    def out_copy(t, n, src, dst):
        z = lax.rem(Z + n + 1, 8)
        return link(
            src.at[span(z, 128)], dst.at[:, cols(Z)], zs.at[t, n + 1], zr.at[t, n + 1], z=z
        )

    @pl.loop(0, 8)
    def _(n):
        z = lax.rem(Z + n + 1, 8)
        for half in range(2):
            i = z * 2 + half
            rows = span(i, 64)
            s = lax.dot_general(qs[i], gathered(i, 0), NT, preferred_element_type=F32) * SCALE
            e = jnp.exp(s - jnp.max(s, axis=-1, keepdims=True))
            p = e / jnp.sum(e, axis=-1, keepdims=True)
            probs[rows, :] = p
            o[rows, :] = jnp.dot(
                p.astype(BF), gathered(i, 16), preferred_element_type=F32
            ).astype(BF)

        @pl.when(n < 7)
        def _():
            out_copy(4, n, o, att).start()

    att_own = pltpu.make_async_copy(o.at[span(Z, 128)], att.at[:, cols(Z)], own_sem.at[4])
    att_own.start()
    att_moved = [out_copy(4, n, o, att) for n in range(7)], att_own
    arrived(g_moved)

    def backward(first, last):
        @pl.loop(first, last)
        def _(n):
            z = lax.rem(Z + n + 1, 8)
            for half in range(2):
                i = z * 2 + half
                rows = span(i, 64)
                q, g, p = qs[i], gs[i], probs[rows, :]
                kg = gathered(i, 0)
                dp = lax.dot_general(g, gathered(i, 16), NT, preferred_element_type=F32)
                delta = jnp.sum(p * dp, axis=-1, keepdims=True)
                ds = (p * (dp - delta)).astype(BF)
                dq[rows, :] = (
                    jnp.dot(ds, kg, preferred_element_type=F32) * SCALE
                ).astype(BF)
                dk = lax.dot_general(ds, q, TN, preferred_element_type=F32)
                dv = lax.dot_general(p.astype(BF), g, TN, preferred_element_type=F32)
                m = n * 2 + half
                for j in range(8):
                    before = tbl[1, m * 8 + j]
                    segk[m * 8 + j] = segk[before] + dk[j * 64 : j * 64 + 64]
                    segv[m * 8 + j] = segv[before] + dv[j * 64 : j * 64 + 64]

            @pl.when(n < 7)
            def _():
                out_copy(5, n, dq, dqo_ref).start()

    backward(0, 8)
    dq_own = pltpu.make_async_copy(dq.at[span(Z, 128)], dqo_ref.at[:, cols(Z)], own_sem.at[5])
    dq_own.start()
    dq_moved = [out_copy(5, n, dq, dqo_ref) for n in range(7)], dq_own
    arrived(att_moved)

    def collect(x, core, t, dst, more=None):
        @pl.loop(0, 8)
        def _(z):
            for half in range(2):
                slot = tbl[2, x * 32 + z * 4 + core * 2 + half]
                rows = slice(half * 64, half * 64 + 64)
                total = segk[slot] * SCALE if t == 0 else segv[slot]
                if more is not None:
                    total += more[z, rows].astype(F32)
                dst[z, rows] = total.astype(BF)

    w_halves, halves, ymoves = {}, {}, {}

    turned[...] = att[...].T

    def share_weight(h, n, y):
        @pl.loop(0, 4)
        def _(m):
            rows = jnp.dot(
                turned[span(m, 256), :], grad[:, cols(y * 2 + h, 256)], preferred_element_type=F32
            ).astype(BF)
            for k in range(16):
                wg[h, k % 2, y, m * 8 + k // 2] = rows[k * 16 : k * 16 + 16]

        w_halves[h, n] = remote(
            wg.at[h, other, y], wr.at[h, y], ws.at[h, n], wrs.at[h, n], c=other
        )

    def share_keys(t):
        for n, x in enumerate((across, right, left, X)):
            collect(x, other, t, given.at[x, t])
            halves[t, n] = remote(given.at[x, t], r.at[x, t], ks.at[t, n], kr.at[t, n], c=other)

    def take(t, n, x):
        halves[t, n].wait_recv()
        collect(x, C, t, a.at[x, t], r.at[x, t])

    first, second = pl.ds(0, 4), pl.ds(4, 4)
    xmoves = {}

    def xsend(name, t, n, src, dst, target):
        xmoves[name, t] = remote(src, dst, xs.at[t, n], xr.at[t, n], x=target)

    def chunk_across(t):
        take(t, 0, across)
        xsend("relay_a", t, 0, a.at[across, t, first], xrel.at[0, t], right)
        xsend("relay_b", t, 1, a.at[across, t, second], xrel.at[1, t], left)

    def chunks_near(t):
        take(t, 1, right)
        xsend("near_a", t, 2, a.at[right, t, second], xin.at[0, t, second], right)
        take(t, 2, left)
        xsend("near_b", t, 3, a.at[left, t, first], xin.at[1, t, first], left)

    def weight_chunk(h, n, y):
        w_halves[h, n].wait_recv()
        add_slabs(wr.at[h, y], wg.at[h, C, y], wr.at[h, y])

    low, high = pl.ds(0, 16), pl.ds(16, 16)

    def ysend(name, h, n, src, dst, target):
        ymoves[name, h] = remote(src, dst, ys.at[h, n], yr.at[h, n], rep=target)

    def weight_far(h):
        weight_chunk(h, 0, far)
        ysend("relay_a", h, 0, wr.at[h, far, low], yrel.at[h, 0], up)
        ysend("relay_b", h, 1, wr.at[h, far, high], yrel.at[h, 1], down)

    def weight_near(h):
        weight_chunk(h, 1, up)
        ysend("near_a", h, 2, wr.at[h, up, high], yin.at[h, 0, high], up)
        weight_chunk(h, 2, down)
        ysend("near_b", h, 3, wr.at[h, down, low], yin.at[h, 1, low], down)

    def weight_last(h):
        ymoves["relay_a", h].wait_recv()
        add_slabs(yrel.at[h, 0], wr.at[h, up, low], yrel.at[h, 0])
        ysend("last_a", h, 4, yrel.at[h, 0], yin.at[h, 0, low], up)
        ymoves["relay_b", h].wait_recv()
        add_slabs(yrel.at[h, 1], wr.at[h, down, high], yrel.at[h, 1])
        ysend("last_b", h, 5, yrel.at[h, 1], yin.at[h, 1, high], down)

    b_moved = {}

    def slabs(h, x):
        return b.at[h, span(x, 8)]

    def weight_rows(h):
        for name in ("near_a", "near_b", "last_a", "last_b"):
            ymoves[name, h].wait_recv()
        add_slabs(b.at[h], wr.at[h, Y], yin.at[h, 0], yin.at[h, 1])
        for d in (1, 3, 2):
            b_moved[h, d] = remote(
                slabs(h, ring(X, d, 4)), xb.at[h, d], bs.at[h, d], br.at[h, d], x=ring(X, d, 4)
            )

    def xpass(t):
        xmoves["relay_a", t].wait_recv()
        add_slabs(xrel.at[0, t], a.at[right, t, first], xrel.at[0, t])
        xsend("last_a", t, 4, xrel.at[0, t], xin.at[0, t, first], right)
        xmoves["relay_b", t].wait_recv()
        add_slabs(xrel.at[1, t], a.at[left, t, second], xrel.at[1, t])
        xsend("last_b", t, 5, xrel.at[1, t], xin.at[1, t, second], left)

    share_weight(0, 0, far)
    share_keys(0)
    weight_far(0)
    chunk_across(0)
    share_weight(0, 1, up)
    share_weight(0, 2, down)
    chunks_near(0)
    weight_near(0)
    share_keys(1)
    share_weight(1, 0, far)
    chunk_across(1)
    weight_far(1)
    chunks_near(1)
    weight_last(0)
    xpass(0)
    share_weight(1, 1, up)
    share_weight(1, 2, down)
    weight_near(1)
    share_weight(0, 3, Y)
    share_weight(1, 3, Y)
    weight_last(1)
    xpass(1)
    weight_chunk(0, 3, Y)
    weight_rows(0)
    weight_chunk(1, 3, Y)
    take(0, 3, X)
    take(1, 3, X)
    mixed[...] = jnp.dot(att[...], weight[...], preferred_element_type=F32).astype(BF)
    mixed_out = pltpu.make_async_copy(mixed, mixed_hbm, in_sem.at[5])
    mixed_out.start()
    early = list(relays.values()) + to_core + list(w_halves.values())
    early += list(halves.values())
    for moved in (k_moved, v_moved, q_moved, g_moved, att_moved, dq_moved):
        early += moved[0]
    for pair in near.values():
        early += pair
    for copy in early:
        copy.wait_send()
    arrived(dq_moved)

    def give(t, src, dst):
        sent = [
            remote(src.at[ring(Z, d, 8)], dst.at[:, cols(Z)], zs.at[t, d], zr.at[t, d],
                   z=ring(Z, d, 8))
            for d in DISTANCES
        ]
        own = pltpu.make_async_copy(src.at[Z], dst.at[:, cols(Z)], own_sem.at[t])
        own.start()
        return sent, own

    def settle(t, dst):
        for name in ("near_a", "near_b", "last_a", "last_b"):
            xmoves[name, t].wait_recv()
        add_slabs(fin.at[t], a.at[X, t], xin.at[0, t], xin.at[1, t])
        return give(6 + t, fin.at[t], dst)

    dk_moved = settle(0, dko_ref)
    weight_rows(1)

    for h in range(2):
        for d in (1, 3, 2):
            b_moved[h, d].wait_recv()

    @pl.loop(0, 8)
    def _(z):
        for h in range(2):
            total = b[h, X * 8 + z].astype(F32)
            for d in (1, 3, 2):
                total += xb[h, d, z].astype(F32)
            c1[z, :, h * 256 : h * 256 + 256] = total.astype(BF)

    c_moved = [
        remote(c1.at[ring(Z, d, 8)], zb.at[d], vs.at[d], vr.at[d], z=ring(Z, d, 8))
        for d in DISTANCES
    ]
    dv_moved = settle(1, dvo_ref)
    for copy in list(xmoves.values()) + list(ymoves.values()) + dk_moved[0]:
        copy.wait_send()
    for copy in c_moved:
        copy.wait_recv()
    total = c1[Z].astype(F32)
    for d in DISTANCES:
        total += zb[d].astype(F32)
    wf[...] = total * (1.0 / math.sqrt(32768))
    w_own = pltpu.make_async_copy(wf, wout_ref.at[:, cols(Y, 512)], in_sem.at[6])
    w_own.start()
    u_moved = [
        remote(wf, wout_ref.at[:, cols(Y, 512)], us.at[d], ur.at[d], rep=ring(Y, d, 4))
        for d in (1, 3, 2)
    ]
    arrived(dk_moved)
    arrived(dv_moved)
    for copy in u_moved:
        copy.wait_recv()
    w_own.wait()
    mixed_out.wait()
    late = dv_moved[0] + list(b_moved.values()) + c_moved + u_moved
    for copy in late:
        copy.wait_send()


OUTPUTS = (
    jax.ShapeDtypeStruct((128, 2048), BF),
    jax.ShapeDtypeStruct((128, 1024), BF),
    jax.ShapeDtypeStruct((128, 1024), BF),
    jax.ShapeDtypeStruct((128, 1024), BF),
    jax.ShapeDtypeStruct((16, 2048), F32),
)


def layer(tables, q, k, v, grad, weight):
    anywhere = pl.BlockSpec(memory_space=pl.ANY)
    dma = pltpu.SemaphoreType.DMA
    vm = pltpu.VMEM
    return pl.pallas_call(
        layer_kernel,
        out_shape=OUTPUTS,
        in_specs=[pl.BlockSpec(memory_space=pltpu.SMEM)] + [anywhere] * 5,
        out_specs=(anywhere,) * 5,
        scratch_shapes=[
            vm((2, BLK, 1024), BF),
            vm((2, BLK, 1024), BF),
            vm((2, BLK, 1024), BF),
            vm((128, 2048), BF),
            vm((1024, 2048), BF),
            vm((2, BLK, 1024), BF),
            vm((256, BLK, HD), BF),
            vm((16, BLK, HD), BF),
            vm((16, BLK, HD), BF),
            vm((1024, 512), F32),
            vm((1024, HD), BF),
            vm((1024, HD), BF),
            vm((128, 1024), BF),
            vm((129, BLK, HD), F32),
            vm((129, BLK, HD), F32),
            vm((4, 2, 8, 128, HD), BF),
            vm((4, 2, 8, 128, HD), BF),
            vm((4, 2, 8, 128, HD), BF),
            vm((2, 2, 8, 128, HD), BF),
            vm((2, 2, 4, 128, HD), BF),
            vm((2, 8, 128, HD), BF),
            vm((2, 2, 4, 32, 16, 256), BF),
            vm((2, 4, 32, 16, 256), BF),
            vm((2, 2, 16, 16, 256), BF),
            vm((2, 2, 32, 16, 256), BF),
            vm((2, 32, 16, 256), BF),
            vm((2, 4, 8, 16, 256), BF),
            vm((8, 16, 512), BF),
            vm((8, 16, 512), BF),
            vm((16, 512), F32),
            vm((128, 2048), BF),
            vm((1024, 128), BF),
            dma((7,)),
            dma((8,)),
            dma((8, 8)),
            dma((8, 8)),
            dma((2, 8, 3)),
            dma((2, 8, 3)),
            dma((2, 11)),
            dma((2, 11)),
            dma((2, 4)),
            dma((2, 4)),
            dma((2, 6)),
            dma((2, 6)),
            dma((2, 4)),
            dma((2, 4)),
            dma((2, 6)),
            dma((2, 6)),
            dma((2, 4)),
            dma((2, 4)),
            dma((8,)),
            dma((8,)),
            dma((4,)),
            dma((4,)),
        ],
        compiler_params=pltpu.CompilerParams(
            collective_id=0, has_side_effects=True, vmem_limit_bytes=63 << 20
        ),
        name="layer",
    )(tables, q, k, v, grad, weight)


def finish_kernel(*refs):
    sources, results, held, sems = refs[:5], refs[5:10], refs[10:15], refs[15]
    taken = [
        pltpu.make_async_copy(src, buf, sems.at[n])
        for n, (src, buf) in enumerate(zip(sources, held))
    ]
    put = [
        pltpu.make_async_copy(buf, dst, sems.at[5 + n])
        for n, (buf, dst) in enumerate(zip(held, results))
    ]
    for copy in taken:
        copy.start()
    for copy, onward in zip(taken, put):
        copy.wait()
        onward.start()
    for copy in put:
        copy.wait()


def finish(arrays):
    anywhere = pl.BlockSpec(memory_space=pl.ANY)
    return pl.pallas_call(
        finish_kernel,
        out_shape=OUTPUTS,
        in_specs=[anywhere] * 5,
        out_specs=(anywhere,) * 5,
        scratch_shapes=[pltpu.VMEM(s.shape, s.dtype) for s in OUTPUTS]
        + [pltpu.SemaphoreType.DMA((10,))],
        compiler_params=pltpu.CompilerParams(vmem_limit_bytes=63 << 20),
        name="finish",
    )(*arrays)


def tables_of(pattern):
    X, Z, C = (lax.axis_index(n) for n in "xzc")
    by_owner = pattern.reshape(4, 8, 2, 16)
    mine = lax.dynamic_slice(by_owner, (X, 0, C, 0), (1, 8, 1, 16)).reshape(8, 16)
    plain = mine.reshape(128)
    turned = jnp.concatenate([mine, mine], axis=0)
    turned = lax.dynamic_slice(turned, (lax.rem(Z + 1, 8), 0), (8, 16)).reshape(128)
    s = plain // 2
    places = ((s % 2) * 4 + s // 16) * 32 + ((s // 2) % 8) * 2 + plain % 2
    order = jnp.arange(128, dtype=jnp.int32)
    same = turned[None, :] == turned[:, None]
    earlier = order[None, :] < order[:, None]
    before = jnp.max(jnp.where(same & earlier, order[None, :], -1), axis=1)
    last = jnp.max(jnp.where(turned[None, :] == order[:, None], order[None, :], -1), axis=1)
    return jnp.stack(
        [places, jnp.where(before < 0, 128, before), jnp.where(last < 0, 128, last)]
    )


def local(query_in, key_in, value_in, out_weight, grad_out, pattern):
    results = layer(
        tables_of(pattern),
        *(a.reshape(2, BLK, 1024) for a in (query_in, key_in, value_in)),
        grad_out[0],
        out_weight,
    )
    mixed_out, query_grad, key_grad, value_grad, weight_grad = finish(results)
    return (mixed_out[None], query_grad[None], key_grad[None], value_grad[None], weight_grad)


def solution(mesh):
    devices = mesh.devices.reshape(4, 8, 2, 4)
    inner = Mesh(devices, ("x", "z", "c", "rep"))
    seq = ("x", "z", "c")
    rows = P("rep", seq, None)
    return jax.shard_map(
        local,
        mesh=inner,
        in_specs=(rows, rows, rows, P(), rows, P()),
        out_specs=(rows, rows, rows, rows, P(seq, None)),
        check_vma=False,
    )
```

```python
import math

import jax
import jax.numpy as jnp
from jax import lax
from jax.experimental import pallas as pl
from jax.experimental.pallas import tpu as pltpu
from jax.sharding import Mesh, PartitionSpec as P

HD = 128
BLK = 64
BF = jnp.bfloat16
F32 = jnp.float32
SCALE = 1.0 / math.sqrt(HD)
DISTANCES = (1, 7, 2, 6, 3, 5, 4)
ARRIVALS = (0,) + DISTANCES
NT = (((1,), (1,)), ((), ()))
TN = (((0,), (0,)), ((), ()))


def ring(value, step, size):
    return lax.rem(value + step + size, size)


def link(src, dst, send, recv, **where):
    return pltpu.make_async_remote_copy(
        src_ref=src,
        dst_ref=dst,
        send_sem=send,
        recv_sem=recv,
        device_id=where,
        device_id_type=pl.DeviceIdType.MESH,
    )


def remote(src, dst, send, recv, **where):
    copy = link(src, dst, send, recv, **where)
    copy.start()
    return copy


def greet(peers):
    barrier = pltpu.get_barrier_semaphore()
    for where in peers:
        pl.semaphore_signal(
            barrier, inc=1, device_id=where, device_id_type=pl.DeviceIdType.MESH
        )
    pl.semaphore_wait(barrier, len(peers))


def span(index, width):
    return pl.ds(pl.multiple_of(index * width, width), width)


def cols(index, width=128):
    return span(index, width)


def add_slabs(dst, first, *more):
    @pl.loop(0, dst.shape[0])
    def _(i):
        total = first[i].astype(F32)
        for ref in more:
            total += ref[i].astype(F32)
        dst[i] = total.astype(dst.dtype)


def layer_kernel(
    tbl, q_hbm, k_hbm, v_hbm, grad_hbm, weight_hbm,
    mixed_hbm, dqo_ref, dko_ref, dvo_ref, wout_ref,
    q_in, k_in, v_in, grad, weight, ag, kv, qs, gs, probs, o, dq, att, segk, segv,
    given, r, a, xin, xrel, fin, wg, wr, yrel, yin, b, xb, c1, zb, wf, mixed, turned, wall,
    in_sem, own_sem, sent, one, zr, fr, kr, xr, wrs, yr,
):
    X, Z, C, Y = (lax.axis_index(n) for n in ("x", "z", "c", "rep"))
    loads = [
        pltpu.make_async_copy(src, dst, in_sem.at[n])
        for n, (src, dst) in enumerate(
            ((k_hbm, k_in), (v_hbm, v_in), (q_hbm, q_in), (grad_hbm, grad), (weight_hbm, weight))
        )
    ]
    for copy in loads:
        copy.start()
    right, left, across, other = ring(X, 1, 4), ring(X, -1, 4), ring(X, 2, 4), 1 - C
    up, down, far = ring(Y, 1, 4), ring(Y, -1, 4), ring(Y, 2, 4)
    greet(
        [{"z": ring(Z, d, 8)} for d in DISTANCES]
        + [{"x": right}, {"x": left}, {"x": across}, {"c": other}]
        + [{"rep": up}, {"rep": down}, {"rep": far}]
    )

    def drain(sem, blocks):
        whole = kv.at[pl.ds(0, blocks)]
        pltpu.make_async_copy(whole, whole, sem).wait()

    def piece(c, x, t, first=0, count=8):
        return kv.at[pl.ds((((c * 4 + x) * 2 + t) * 8 + first) * 2, count * 2)]

    targets = (
        lambda: piece(C, X, 0, Z, 1),
        lambda: piece(C, X, 1, Z, 1),
        lambda: qs.at[pl.ds(Z * 2, 2)],
        lambda: gs.at[pl.ds(Z * 2, 2)],
    )

    def spread(t, src):
        arriving = [
            remote(
                src.at[:, :, cols(ring(Z, d, 8))], targets[t](), sent.at[0],
                zr.at[t, d - 1] if t < 2 else one.at[t],
                z=ring(Z, d, 8),
            )
            for d in DISTANCES
        ]
        own = pltpu.make_async_copy(src.at[:, :, cols(Z)], targets[t](), own_sem.at[t])
        own.start()
        return arriving, own

    def arrived(t, own):
        own.wait()
        drain(one.at[t], 14)

    loads[0].wait()
    k_moved = spread(0, k_in)
    loads[1].wait()
    v_moved = spread(1, v_in)
    loads[2].wait()
    q_moved = spread(2, q_in)
    segk[128] = jnp.zeros((BLK, HD), F32)
    segv[128] = jnp.zeros((BLK, HD), F32)
    loads[3].wait()
    loads[4].wait()
    rows = lax.dot_general(grad[...], weight[...], NT, preferred_element_type=F32).astype(BF)
    ag[0] = rows[:64]
    ag[1] = rows[64:]
    g_moved = spread(3, ag)

    near, relays = {}, {}

    def send_near(t, d):
        if d == 0:
            moves[t][1].wait()
        else:
            moves[t][0][DISTANCES.index(d)].wait_recv()
        here = piece(C, X, t, ring(Z, -d, 8), 1)
        near[t, d] = (
            remote(here, here, sent.at[0], fr.at[t, d, 0], x=right),
            remote(here, here, sent.at[0], fr.at[t, d, 1], x=left),
        )

    def send_relay(t, d):
        for copy in near[t, d]:
            copy.wait_recv()
        source, target = (left, right) if d < 4 else (right, left)
        here = piece(C, source, t, ring(Z, -d, 8), 1)
        relays[t, d] = remote(here, here, sent.at[0], fr.at[t, d, 2], x=target)

    def across_core(t, n, x):
        here = piece(C, x, t)
        remote(here, here, sent.at[1], one.at[0], c=other)

    moves = (k_moved, v_moved)
    steps = [(t, d) for t in range(2) for d in ARRIVALS]
    for n in range(len(steps) + 4):
        if n < len(steps):
            send_near(*steps[n])
            if n % 8 == 7:
                across_core(n // 8, 0, X)
        if n >= 4:
            send_relay(*steps[n - 4])
            if n % 8 == 3:
                across_core(n // 8 - 1, 1, left)
                across_core(n // 8 - 1, 2, right)
    for t in range(2):
        for d in ARRIVALS:
            relays[t, d].wait_recv()
            here = piece(C, across, t, ring(Z, -d, 8), 1)
            remote(here, here, sent.at[1], one.at[0], c=other)
    arrived(2, q_moved[1])
    drain(one.at[0], 128)

    def gathered(m, extra):
        return jnp.concatenate(
            [
                kv[tbl[0, j * 16 + m] + extra]
                for j in range(8)
            ],
            axis=0,
        )

    def out_copy(t, n, src, dst):
        z = lax.rem(Z + n + 1, 8)
        return link(
            src.at[span(z, 128)], dst.at[:, cols(Z)], sent.at[2], one.at[t], z=z
        )

    @pl.loop(0, 8)
    def _(n):
        z = lax.rem(Z + n + 1, 8)
        for half in range(2):
            i, m = z * 2 + half, n * 2 + half
            rows = span(i, 64)
            s = lax.dot_general(qs[i], gathered(m, 0), NT, preferred_element_type=F32) * SCALE
            e = jnp.exp(s - jnp.max(s, axis=-1, keepdims=True))
            p = e / jnp.sum(e, axis=-1, keepdims=True)
            probs[rows, :] = p
            o[rows, :] = jnp.dot(
                p.astype(BF), gathered(m, 16), preferred_element_type=F32
            ).astype(BF)

        @pl.when(n < 7)
        def _():
            out_copy(4, n, o, att).start()

    att_own = pltpu.make_async_copy(o.at[span(Z, 128)], att.at[:, cols(Z)], own_sem.at[4])
    att_own.start()
    arrived(3, g_moved[1])

    def backward(first, last):
        @pl.loop(first, last)
        def _(n):
            z = lax.rem(Z + n + 1, 8)
            for half in range(2):
                i, m = z * 2 + half, n * 2 + half
                rows = span(i, 64)
                q, g, p = qs[i], gs[i], probs[rows, :]
                kg = gathered(m, 0)
                dp = lax.dot_general(g, gathered(m, 16), NT, preferred_element_type=F32)
                delta = jnp.sum(p * dp, axis=-1, keepdims=True)
                ds = (p * (dp - delta)).astype(BF)
                dq[rows, :] = (
                    jnp.dot(ds, kg, preferred_element_type=F32) * SCALE
                ).astype(BF)
                dk = lax.dot_general(ds, q, TN, preferred_element_type=F32)
                dv = lax.dot_general(p.astype(BF), g, TN, preferred_element_type=F32)
                for j in range(8):
                    before = tbl[1, j * 16 + m]
                    segk[j * 16 + m] = segk[before] + dk[j * 64 : j * 64 + 64]
                    segv[j * 16 + m] = segv[before] + dv[j * 64 : j * 64 + 64]

            @pl.when(n < 7)
            def _():
                out_copy(5, n, dq, dqo_ref).start()

    backward(0, 8)
    dq_own = pltpu.make_async_copy(dq.at[span(Z, 128)], dqo_ref.at[:, cols(Z)], own_sem.at[5])
    dq_own.start()
    arrived(4, att_own)

    def collect(x, core, t, dst, more=None):
        @pl.loop(0, 8)
        def _(z):
            for half in range(2):
                slot = tbl[2, x * 32 + z * 4 + core * 2 + half]
                rows = slice(half * 64, half * 64 + 64)
                total = segk[slot] * SCALE if t == 0 else segv[slot]
                if more is not None:
                    total += more[z, rows].astype(F32)
                dst[z, rows] = total.astype(BF)

    w_halves, halves, ymoves = {}, {}, {}

    turned[...] = att[...].T

    def share_weight(h, n, y):
        @pl.loop(0, 4)
        def _(m):
            rows = jnp.dot(
                turned[span(m, 256), :], grad[:, cols(y * 2 + h, 256)], preferred_element_type=F32
            ).astype(BF)
            for k in range(16):
                wg[h, k % 2, y, m * 8 + k // 2] = rows[k * 16 : k * 16 + 16]

        w_halves[h, n] = remote(
            wg.at[h, other, y], wr.at[h, y], sent.at[2], wrs.at[h, n], c=other
        )

    def share_keys(t):
        for n, x in enumerate((across, right, left, X)):
            collect(x, other, t, given.at[x, t])
            halves[t, n] = remote(given.at[x, t], r.at[x, t], sent.at[3], kr.at[t, n], c=other)

    def take(t, n, x):
        halves[t, n].wait_recv()
        collect(x, C, t, a.at[x, t], r.at[x, t])

    first, second = pl.ds(0, 4), pl.ds(4, 4)
    xmoves = {}

    def xsend(name, t, n, src, dst, target):
        xmoves[name, t] = remote(src, dst, sent.at[4], xr.at[t, n], x=target)

    def chunk_across(t):
        take(t, 0, across)
        xsend("relay_a", t, 0, a.at[across, t, first], xrel.at[0, t], right)
        xsend("relay_b", t, 1, a.at[across, t, second], xrel.at[1, t], left)

    def chunks_near(t):
        take(t, 1, right)
        xsend("near_a", t, 2, a.at[right, t, second], xin.at[0, t, second], right)
        take(t, 2, left)
        xsend("near_b", t, 3, a.at[left, t, first], xin.at[1, t, first], left)

    def weight_chunk(h, n, y):
        w_halves[h, n].wait_recv()
        add_slabs(wr.at[h, y], wg.at[h, C, y], wr.at[h, y])

    low, high = pl.ds(0, 16), pl.ds(16, 16)

    def ysend(name, h, n, src, dst, target):
        ymoves[name, h] = remote(src, dst, sent.at[4], yr.at[h, n], rep=target)

    def weight_far(h):
        weight_chunk(h, 0, far)
        ysend("relay_a", h, 0, wr.at[h, far, low], yrel.at[h, 0], up)
        ysend("relay_b", h, 1, wr.at[h, far, high], yrel.at[h, 1], down)

    def weight_near(h):
        weight_chunk(h, 1, up)
        ysend("near_a", h, 2, wr.at[h, up, high], yin.at[h, 0, high], up)
        weight_chunk(h, 2, down)
        ysend("near_b", h, 3, wr.at[h, down, low], yin.at[h, 1, low], down)

    def weight_last(h):
        ymoves["relay_a", h].wait_recv()
        add_slabs(yrel.at[h, 0], wr.at[h, up, low], yrel.at[h, 0])
        ysend("last_a", h, 4, yrel.at[h, 0], yin.at[h, 0, low], up)
        ymoves["relay_b", h].wait_recv()
        add_slabs(yrel.at[h, 1], wr.at[h, down, high], yrel.at[h, 1])
        ysend("last_b", h, 5, yrel.at[h, 1], yin.at[h, 1, high], down)

    def slabs(h, x):
        return b.at[h, span(x, 8)]

    def weight_rows(h):
        for name in ("near_a", "near_b", "last_a", "last_b"):
            ymoves[name, h].wait_recv()
        add_slabs(b.at[h], wr.at[h, Y], yin.at[h, 0], yin.at[h, 1])
        for d in (1, 3, 2):
            remote(
                slabs(h, ring(X, d, 4)), xb.at[h, d], sent.at[5], one.at[1], x=ring(X, d, 4)
            )

    def xpass(t):
        xmoves["relay_a", t].wait_recv()
        add_slabs(xrel.at[0, t], a.at[right, t, first], xrel.at[0, t])
        xsend("last_a", t, 4, xrel.at[0, t], xin.at[0, t, first], right)
        xmoves["relay_b", t].wait_recv()
        add_slabs(xrel.at[1, t], a.at[left, t, second], xrel.at[1, t])
        xsend("last_b", t, 5, xrel.at[1, t], xin.at[1, t, second], left)

    share_weight(0, 0, far)
    share_keys(0)
    weight_far(0)
    chunk_across(0)
    share_weight(0, 1, up)
    share_weight(0, 2, down)
    chunks_near(0)
    weight_near(0)
    share_keys(1)
    share_weight(1, 0, far)
    chunk_across(1)
    weight_far(1)
    chunks_near(1)
    weight_last(0)
    xpass(0)
    share_weight(1, 1, up)
    share_weight(1, 2, down)
    weight_near(1)
    share_weight(0, 3, Y)
    share_weight(1, 3, Y)
    weight_last(1)
    xpass(1)
    weight_chunk(0, 3, Y)
    weight_rows(0)
    weight_chunk(1, 3, Y)
    take(0, 3, X)
    take(1, 3, X)
    mixed[...] = jnp.dot(att[...], weight[...], preferred_element_type=F32).astype(BF)
    mixed_out = pltpu.make_async_copy(mixed, mixed_hbm, in_sem.at[5])
    mixed_out.start()
    for n, blocks in enumerate((152, 128, 156, 128)):
        drain(sent.at[n], blocks)
    arrived(5, dq_own)

    def give(t, src, dst, distances):
        for d in distances:
            remote(
                src.at[ring(Z, d, 8)], dst.at[:, cols(Z)], sent.at[5], one.at[t],
                z=ring(Z, d, 8),
            )

    def settle(t, dst, distances):
        for name in ("near_a", "near_b", "last_a", "last_b"):
            xmoves[name, t].wait_recv()
        add_slabs(fin.at[t], a.at[X, t], xin.at[0, t], xin.at[1, t])
        own = pltpu.make_async_copy(fin.at[t, Z], dst.at[:, cols(Z)], own_sem.at[6 + t])
        own.start()
        give(6 + t, fin.at[t], dst, distances)
        return own

    dk_own = settle(0, dko_ref, DISTANCES)
    weight_rows(1)
    dv_own = settle(1, dvo_ref, (4, 3, 5, 2))

    drain(one.at[1], 24)

    @pl.loop(0, 8)
    def _(z):
        for h in range(2):
            total = b[h, X * 8 + z].astype(F32)
            for d in (1, 3, 2):
                total += xb[h, d, z].astype(F32)
            c1[z, :, h * 256 : h * 256 + 256] = total.astype(BF)

    for d in DISTANCES:
        remote(c1.at[ring(Z, d, 8)], zb.at[d], sent.at[5], one.at[8], z=ring(Z, d, 8))
    give(7, fin.at[1], dvo_ref, (6, 1, 7))
    drain(sent.at[4], 192)
    drain(one.at[8], 7)
    total = c1[Z].astype(F32)
    for d in DISTANCES:
        total += zb[d].astype(F32)
    wf[...] = total * (1.0 / math.sqrt(32768))
    wall[:, cols(Y, 512)] = wf[...]
    for d in (1, 3, 2):
        remote(wf, wall.at[:, cols(Y, 512)], sent.at[5], one.at[9], rep=ring(Y, d, 4))
    drain(one.at[9], 6)
    w_own = pltpu.make_async_copy(wall, wout_ref, in_sem.at[6])
    w_own.start()
    arrived(6, dk_own)
    arrived(7, dv_own)
    mixed_out.wait()
    drain(sent.at[5], 65)
    w_own.wait()


OUTPUTS = (
    jax.ShapeDtypeStruct((128, 2048), BF),
    jax.ShapeDtypeStruct((128, 1024), BF),
    jax.ShapeDtypeStruct((128, 1024), BF),
    jax.ShapeDtypeStruct((128, 1024), BF),
    jax.ShapeDtypeStruct((16, 2048), F32),
)


def layer(tables, q, k, v, grad, weight):
    anywhere = pl.BlockSpec(memory_space=pl.ANY)
    dma = pltpu.SemaphoreType.DMA
    vm = pltpu.VMEM
    return pl.pallas_call(
        layer_kernel,
        out_shape=OUTPUTS,
        in_specs=[pl.BlockSpec(memory_space=pltpu.SMEM)] + [anywhere] * 5,
        out_specs=(anywhere,) * 5,
        scratch_shapes=[
            vm((2, BLK, 1024), BF),
            vm((2, BLK, 1024), BF),
            vm((2, BLK, 1024), BF),
            vm((128, 2048), BF),
            vm((1024, 2048), BF),
            vm((2, BLK, 1024), BF),
            vm((256, BLK, HD), BF),
            vm((16, BLK, HD), BF),
            vm((16, BLK, HD), BF),
            vm((1024, 512), F32),
            vm((1024, HD), BF),
            vm((1024, HD), BF),
            vm((128, 1024), BF),
            vm((129, BLK, HD), F32),
            vm((129, BLK, HD), F32),
            vm((4, 2, 8, 128, HD), BF),
            vm((4, 2, 8, 128, HD), BF),
            vm((4, 2, 8, 128, HD), BF),
            vm((2, 2, 8, 128, HD), BF),
            vm((2, 2, 4, 128, HD), BF),
            vm((2, 8, 128, HD), BF),
            vm((2, 2, 4, 32, 16, 256), BF),
            vm((2, 4, 32, 16, 256), BF),
            vm((2, 2, 16, 16, 256), BF),
            vm((2, 2, 32, 16, 256), BF),
            vm((2, 32, 16, 256), BF),
            vm((2, 4, 8, 16, 256), BF),
            vm((8, 16, 512), BF),
            vm((8, 16, 512), BF),
            vm((16, 512), F32),
            vm((128, 2048), BF),
            vm((1024, 128), BF),
            vm((16, 2048), F32),
            dma((7,)),
            dma((8,)),
            dma((6,)),
            dma((10,)),
            dma((2, 7)),
            dma((2, 8, 3)),
            dma((2, 4)),
            dma((2, 6)),
            dma((2, 4)),
            dma((2, 6)),
        ],
        compiler_params=pltpu.CompilerParams(
            collective_id=0, has_side_effects=True, vmem_limit_bytes=63 << 20
        ),
        name="layer",
    )(tables, q, k, v, grad, weight)


def finish_kernel(*refs):
    sources, results, held, sems = refs[:5], refs[5:10], refs[10:15], refs[15]
    taken = [
        pltpu.make_async_copy(src, buf, sems.at[n])
        for n, (src, buf) in enumerate(zip(sources, held))
    ]
    put = [
        pltpu.make_async_copy(buf, dst, sems.at[5 + n])
        for n, (buf, dst) in enumerate(zip(held, results))
    ]
    for copy in taken:
        copy.start()
    for copy, onward in zip(taken, put):
        copy.wait()
        onward.start()
    for copy in put:
        copy.wait()


def finish(arrays):
    anywhere = pl.BlockSpec(memory_space=pl.ANY)
    return pl.pallas_call(
        finish_kernel,
        out_shape=OUTPUTS,
        in_specs=[anywhere] * 5,
        out_specs=(anywhere,) * 5,
        scratch_shapes=[pltpu.VMEM(s.shape, s.dtype) for s in OUTPUTS]
        + [pltpu.SemaphoreType.DMA((10,))],
        compiler_params=pltpu.CompilerParams(vmem_limit_bytes=63 << 20),
        name="finish",
    )(*arrays)


def tables_of(pattern):
    X, Z, C = (lax.axis_index(n) for n in "xzc")
    m = jnp.arange(16, dtype=jnp.int32)
    t = jnp.arange(128, dtype=jnp.int32)
    rows = X * 32 + ((Z + 1 + (m >> 1)) & 7) * 4 + C * 2 + (m & 1)
    chosen = rows[None, :, None] == t[None, None, :]
    mine = jnp.sum(jnp.where(chosen, pattern.T[:, None, :], 0), axis=2).reshape(128)
    s = mine >> 1
    places = ((s & 1) * 4 + (s >> 4)) * 32 + ((s >> 1) & 7) * 2 + (mine & 1)
    order = (t & 15) * 8 + (t >> 4)
    same = mine[None, :] == mine[:, None]
    earlier = order[None, :] < order[:, None]
    before = jnp.max(jnp.where(same & earlier, order[None, :], -1), axis=1)
    last = jnp.max(jnp.where(mine[None, :] == t[:, None], order[None, :], -1), axis=1)
    links = jnp.stack([before, last])
    links = jnp.where(links < 0, 128, (links & 7) * 16 + (links >> 3))
    return jnp.concatenate([places[None], links])


def local(query_in, key_in, value_in, out_weight, grad_out, pattern):
    results = layer(
        tables_of(pattern),
        *(a.reshape(2, BLK, 1024) for a in (query_in, key_in, value_in)),
        grad_out[0],
        out_weight,
    )
    mixed_out, query_grad, key_grad, value_grad, weight_grad = finish(results)
    return (mixed_out[None], query_grad[None], key_grad[None], value_grad[None], weight_grad)


def solution(mesh):
    devices = mesh.devices.reshape(4, 8, 2, 4)
    inner = Mesh(devices, ("x", "z", "c", "rep"))
    seq = ("x", "z", "c")
    rows = P("rep", seq, None)
    return jax.shard_map(
        local,
        mesh=inner,
        in_specs=(rows, rows, rows, P(), rows, P()),
        out_specs=(rows, rows, rows, rows, P(seq, None)),
        check_vma=False,
    )
```

```python
import math

import jax
import jax.numpy as jnp
from jax import lax
from jax.experimental import pallas as pl
from jax.experimental.pallas import tpu as pltpu
from jax.sharding import Mesh, PartitionSpec as P

HD = 128
BLK = 64
BF = jnp.bfloat16
F32 = jnp.float32
SCALE = 1.0 / math.sqrt(HD)
DISTANCES = (1, 7, 2, 6, 3, 5, 4)
ARRIVALS = (0,) + DISTANCES
NT = (((1,), (1,)), ((), ()))
TN = (((0,), (0,)), ((), ()))


def ring(value, step, size):
    return lax.rem(value + step + size, size)


def link(src, dst, send, recv, **where):
    return pltpu.make_async_remote_copy(
        src_ref=src,
        dst_ref=dst,
        send_sem=send,
        recv_sem=recv,
        device_id=where,
        device_id_type=pl.DeviceIdType.MESH,
    )


def remote(src, dst, send, recv, **where):
    copy = link(src, dst, send, recv, **where)
    copy.start()
    return copy


def greet(peers):
    barrier = pltpu.get_barrier_semaphore()
    for where in peers:
        pl.semaphore_signal(
            barrier, inc=1, device_id=where, device_id_type=pl.DeviceIdType.MESH
        )
    pl.semaphore_wait(barrier, len(peers))


def span(index, width):
    return pl.ds(pl.multiple_of(index * width, width), width)


def cols(index, width=128):
    return span(index, width)


def add_slabs(dst, first, *more):
    @pl.loop(0, dst.shape[0])
    def _(i):
        total = first[i].astype(F32)
        for ref in more:
            total += ref[i].astype(F32)
        dst[i] = total.astype(dst.dtype)


def layer_kernel(
    tbl, q_hbm, k_hbm, v_hbm, grad_hbm, weight_hbm,
    mixed_hbm, dqo_ref, dko_ref, dvo_ref, wout_ref,
    q_in, k_in, v_in, grad, weight, ag, kv, qs, gs, probs, o, dq, att, segk, segv,
    given, r, a, xin, xrel, fin, wg, wr, yrel, yin, b, xb, c1, zb, wf, mixed, turned, wall,
    in_sem, own_sem, sent, one, zr, fr, kr, xr, wrs, yr,
):
    X, Z, C, Y = (lax.axis_index(n) for n in ("x", "z", "c", "rep"))
    loads = [
        pltpu.make_async_copy(src, dst, in_sem.at[n])
        for n, (src, dst) in enumerate(
            ((k_hbm, k_in), (v_hbm, v_in), (q_hbm, q_in), (grad_hbm, grad), (weight_hbm, weight))
        )
    ]
    for copy in loads:
        copy.start()
    right, left, across, other = ring(X, 1, 4), ring(X, -1, 4), ring(X, 2, 4), 1 - C
    up, down, far = ring(Y, 1, 4), ring(Y, -1, 4), ring(Y, 2, 4)
    greet(
        [{"z": ring(Z, d, 8)} for d in DISTANCES]
        + [{"x": right}, {"x": left}, {"x": across}, {"c": other}]
        + [{"rep": up}, {"rep": down}, {"rep": far}]
    )

    def drain(sem, blocks):
        whole = kv.at[pl.ds(0, blocks)]
        pltpu.make_async_copy(whole, whole, sem).wait()

    def piece(c, x, t, first=0, count=8):
        return kv.at[pl.ds((((c * 4 + x) * 2 + t) * 8 + first) * 2, count * 2)]

    targets = (
        lambda: piece(C, X, 0, Z, 1),
        lambda: piece(C, X, 1, Z, 1),
        lambda: qs.at[pl.ds(Z * 2, 2)],
        lambda: gs.at[pl.ds(Z * 2, 2)],
    )

    def spread(t, src):
        arriving = [
            remote(
                src.at[:, :, cols(ring(Z, d, 8))], targets[t](), sent.at[0],
                zr.at[t, d - 1] if t < 2 else one.at[t],
                z=ring(Z, d, 8),
            )
            for d in DISTANCES
        ]
        own = pltpu.make_async_copy(src.at[:, :, cols(Z)], targets[t](), own_sem.at[t])
        own.start()
        return arriving, own

    def arrived(t, own):
        own.wait()
        drain(one.at[t], 14)

    loads[0].wait()
    k_moved = spread(0, k_in)
    loads[1].wait()
    v_moved = spread(1, v_in)
    loads[2].wait()
    q_moved = spread(2, q_in)
    segk[128] = jnp.zeros((BLK, HD), F32)
    segv[128] = jnp.zeros((BLK, HD), F32)
    loads[3].wait()
    loads[4].wait()
    rows = lax.dot_general(grad[...], weight[...], NT, preferred_element_type=F32).astype(BF)
    ag[0] = rows[:64]
    ag[1] = rows[64:]
    g_moved = spread(3, ag)

    near, relays = {}, {}

    def send_near(t, d):
        if d == 0:
            moves[t][1].wait()
        else:
            moves[t][0][DISTANCES.index(d)].wait_recv()
        here = piece(C, X, t, ring(Z, -d, 8), 1)
        near[t, d] = (
            remote(here, here, sent.at[0], fr.at[t, d, 0], x=right),
            remote(here, here, sent.at[0], fr.at[t, d, 1], x=left),
        )

    def send_relay(t, d):
        for copy in near[t, d]:
            copy.wait_recv()
        source, target = (left, right) if d < 4 else (right, left)
        here = piece(C, source, t, ring(Z, -d, 8), 1)
        relays[t, d] = remote(here, here, sent.at[0], fr.at[t, d, 2], x=target)

    def across_core(t, n, x):
        here = piece(C, x, t)
        remote(here, here, sent.at[1], one.at[0], c=other)

    moves = (k_moved, v_moved)
    steps = [(t, d) for t in range(2) for d in ARRIVALS]
    for n in range(len(steps) + 6):
        if n < len(steps):
            send_near(*steps[n])
            if n % 8 == 7:
                across_core(n // 8, 0, X)
        if n >= 6:
            send_relay(*steps[n - 6])
            if n % 8 == 5:
                across_core(n // 8 - 1, 1, left)
                across_core(n // 8 - 1, 2, right)
    for t in range(2):
        for d in ARRIVALS:
            relays[t, d].wait_recv()
            here = piece(C, across, t, ring(Z, -d, 8), 1)
            remote(here, here, sent.at[1], one.at[0], c=other)
    arrived(2, q_moved[1])
    drain(one.at[0], 128)

    def gathered(m, extra):
        return jnp.concatenate(
            [
                kv[tbl[0, j * 16 + m] + extra]
                for j in range(8)
            ],
            axis=0,
        )

    def out_copy(t, n, src, dst):
        z = lax.rem(Z + n + 1, 8)
        return link(
            src.at[span(z, 128)], dst.at[:, cols(Z)], sent.at[2], one.at[t], z=z
        )

    @pl.loop(0, 8)
    def _(n):
        z = lax.rem(Z + n + 1, 8)
        for half in range(2):
            i, m = z * 2 + half, n * 2 + half
            rows = span(i, 64)
            s = lax.dot_general(qs[i], gathered(m, 0), NT, preferred_element_type=F32) * SCALE
            e = jnp.exp(s - jnp.max(s, axis=-1, keepdims=True))
            p = e / jnp.sum(e, axis=-1, keepdims=True)
            probs[rows, :] = p
            o[rows, :] = jnp.dot(
                p.astype(BF), gathered(m, 16), preferred_element_type=F32
            ).astype(BF)

        @pl.when(n < 7)
        def _():
            out_copy(4, n, o, att).start()

    att_own = pltpu.make_async_copy(o.at[span(Z, 128)], att.at[:, cols(Z)], own_sem.at[4])
    att_own.start()
    arrived(3, g_moved[1])

    def backward(first, last):
        @pl.loop(first, last)
        def _(n):
            z = lax.rem(Z + n + 1, 8)
            for half in range(2):
                i, m = z * 2 + half, n * 2 + half
                rows = span(i, 64)
                q, g, p = qs[i], gs[i], probs[rows, :]
                kg = gathered(m, 0)
                dp = lax.dot_general(g, gathered(m, 16), NT, preferred_element_type=F32)
                delta = jnp.sum(p * dp, axis=-1, keepdims=True)
                ds = (p * (dp - delta)).astype(BF)
                dq[rows, :] = (
                    jnp.dot(ds, kg, preferred_element_type=F32) * SCALE
                ).astype(BF)
                dk = lax.dot_general(ds, q, TN, preferred_element_type=F32)
                dv = lax.dot_general(p.astype(BF), g, TN, preferred_element_type=F32)
                for j in range(8):
                    before = tbl[1, j * 16 + m]
                    segk[j * 16 + m] = segk[before] + dk[j * 64 : j * 64 + 64]
                    segv[j * 16 + m] = segv[before] + dv[j * 64 : j * 64 + 64]

            @pl.when(n < 7)
            def _():
                out_copy(5, n, dq, dqo_ref).start()

    backward(0, 8)
    dq_own = pltpu.make_async_copy(dq.at[span(Z, 128)], dqo_ref.at[:, cols(Z)], own_sem.at[5])
    dq_own.start()
    arrived(4, att_own)

    def collect(x, core, t, dst, more=None):
        @pl.loop(0, 8)
        def _(z):
            for half in range(2):
                slot = tbl[2, x * 32 + z * 4 + core * 2 + half]
                rows = slice(half * 64, half * 64 + 64)
                total = segk[slot] * SCALE if t == 0 else segv[slot]
                if more is not None:
                    total += more[z, rows].astype(F32)
                dst[z, rows] = total.astype(BF)

    w_halves, halves, ymoves = {}, {}, {}

    turned[...] = att[...].T

    def share_weight(h, n, y):
        @pl.loop(0, 4)
        def _(m):
            rows = jnp.dot(
                turned[span(m, 256), :], grad[:, cols(y * 2 + h, 256)], preferred_element_type=F32
            ).astype(BF)
            for k in range(16):
                wg[h, k % 2, y, m * 8 + k // 2] = rows[k * 16 : k * 16 + 16]

        w_halves[h, n] = remote(
            wg.at[h, other, y], wr.at[h, y], sent.at[2], wrs.at[h, n], c=other
        )

    def share_keys(t):
        for n, x in enumerate((across, right, left, X)):
            collect(x, other, t, given.at[x, t])
            halves[t, n] = remote(given.at[x, t], r.at[x, t], sent.at[3], kr.at[t, n], c=other)

    def take(t, n, x):
        halves[t, n].wait_recv()
        collect(x, C, t, a.at[x, t], r.at[x, t])

    first, second = pl.ds(0, 4), pl.ds(4, 4)
    xmoves = {}

    def xsend(name, t, n, src, dst, target):
        xmoves[name, t] = remote(src, dst, sent.at[4], xr.at[t, n], x=target)

    def chunk_across(t):
        take(t, 0, across)
        xsend("relay_a", t, 0, a.at[across, t, first], xrel.at[0, t], right)
        xsend("relay_b", t, 1, a.at[across, t, second], xrel.at[1, t], left)

    def chunks_near(t):
        take(t, 1, right)
        xsend("near_a", t, 2, a.at[right, t, second], xin.at[0, t, second], right)
        take(t, 2, left)
        xsend("near_b", t, 3, a.at[left, t, first], xin.at[1, t, first], left)

    def weight_chunk(h, n, y):
        w_halves[h, n].wait_recv()
        add_slabs(wr.at[h, y], wg.at[h, C, y], wr.at[h, y])

    low, high = pl.ds(0, 16), pl.ds(16, 16)

    def ysend(name, h, n, src, dst, target):
        ymoves[name, h] = remote(src, dst, sent.at[4], yr.at[h, n], rep=target)

    def weight_far(h):
        weight_chunk(h, 0, far)
        ysend("relay_a", h, 0, wr.at[h, far, low], yrel.at[h, 0], up)
        ysend("relay_b", h, 1, wr.at[h, far, high], yrel.at[h, 1], down)

    def weight_near(h):
        weight_chunk(h, 1, up)
        ysend("near_a", h, 2, wr.at[h, up, high], yin.at[h, 0, high], up)
        weight_chunk(h, 2, down)
        ysend("near_b", h, 3, wr.at[h, down, low], yin.at[h, 1, low], down)

    def weight_last(h):
        ymoves["relay_a", h].wait_recv()
        add_slabs(yrel.at[h, 0], wr.at[h, up, low], yrel.at[h, 0])
        ysend("last_a", h, 4, yrel.at[h, 0], yin.at[h, 0, low], up)
        ymoves["relay_b", h].wait_recv()
        add_slabs(yrel.at[h, 1], wr.at[h, down, high], yrel.at[h, 1])
        ysend("last_b", h, 5, yrel.at[h, 1], yin.at[h, 1, high], down)

    def slabs(h, x):
        return b.at[h, span(x, 8)]

    def weight_rows(h):
        for name in ("near_a", "near_b", "last_a", "last_b"):
            ymoves[name, h].wait_recv()
        add_slabs(b.at[h], wr.at[h, Y], yin.at[h, 0], yin.at[h, 1])
        for d in (1, 3, 2):
            remote(
                slabs(h, ring(X, d, 4)), xb.at[h, d], sent.at[5], one.at[1], x=ring(X, d, 4)
            )

    def xpass(t):
        xmoves["relay_a", t].wait_recv()
        add_slabs(xrel.at[0, t], a.at[right, t, first], xrel.at[0, t])
        xsend("last_a", t, 4, xrel.at[0, t], xin.at[0, t, first], right)
        xmoves["relay_b", t].wait_recv()
        add_slabs(xrel.at[1, t], a.at[left, t, second], xrel.at[1, t])
        xsend("last_b", t, 5, xrel.at[1, t], xin.at[1, t, second], left)

    share_weight(0, 0, far)
    share_keys(0)
    weight_far(0)
    chunk_across(0)
    share_weight(0, 1, up)
    share_weight(0, 2, down)
    chunks_near(0)
    weight_near(0)
    share_keys(1)
    share_weight(1, 0, far)
    chunk_across(1)
    weight_far(1)
    chunks_near(1)
    weight_last(0)
    xpass(0)
    share_weight(1, 1, up)
    share_weight(1, 2, down)
    weight_near(1)
    share_weight(0, 3, Y)
    share_weight(1, 3, Y)
    weight_last(1)
    xpass(1)
    weight_chunk(0, 3, Y)
    weight_rows(0)
    weight_chunk(1, 3, Y)
    take(0, 3, X)
    take(1, 3, X)
    mixed[...] = jnp.dot(att[...], weight[...], preferred_element_type=F32).astype(BF)
    mixed_out = pltpu.make_async_copy(mixed, mixed_hbm, in_sem.at[5])
    mixed_out.start()
    for n, blocks in enumerate((152, 128, 156, 128)):
        drain(sent.at[n], blocks)
    arrived(5, dq_own)

    def give(t, src, dst, distances):
        for d in distances:
            remote(
                src.at[ring(Z, d, 8)], dst.at[:, cols(Z)], sent.at[5], one.at[t],
                z=ring(Z, d, 8),
            )

    def settle(t, dst, distances):
        for name in ("near_a", "near_b", "last_a", "last_b"):
            xmoves[name, t].wait_recv()
        add_slabs(fin.at[t], a.at[X, t], xin.at[0, t], xin.at[1, t])
        own = pltpu.make_async_copy(fin.at[t, Z], dst.at[:, cols(Z)], own_sem.at[6 + t])
        own.start()
        give(6 + t, fin.at[t], dst, distances)
        return own

    dk_own = settle(0, dko_ref, DISTANCES)
    weight_rows(1)
    dv_own = settle(1, dvo_ref, (4, 3, 5, 2))

    drain(one.at[1], 24)

    @pl.loop(0, 8)
    def _(z):
        for h in range(2):
            total = b[h, X * 8 + z].astype(F32)
            for d in (1, 3, 2):
                total += xb[h, d, z].astype(F32)
            c1[z, :, h * 256 : h * 256 + 256] = total.astype(BF)

    for d in DISTANCES:
        remote(c1.at[ring(Z, d, 8)], zb.at[d], sent.at[5], one.at[8], z=ring(Z, d, 8))
    give(7, fin.at[1], dvo_ref, (6, 1, 7))
    drain(sent.at[4], 192)
    drain(one.at[8], 7)
    total = c1[Z].astype(F32)
    for d in DISTANCES:
        total += zb[d].astype(F32)
    wf[...] = total * (1.0 / math.sqrt(32768))
    wall[:, cols(Y, 512)] = wf[...]
    for d in (1, 3, 2):
        remote(wf, wall.at[:, cols(Y, 512)], sent.at[5], one.at[9], rep=ring(Y, d, 4))
    drain(one.at[9], 6)
    w_own = pltpu.make_async_copy(wall, wout_ref, in_sem.at[6])
    w_own.start()
    arrived(6, dk_own)
    arrived(7, dv_own)
    mixed_out.wait()
    drain(sent.at[5], 65)
    w_own.wait()


OUTPUTS = (
    jax.ShapeDtypeStruct((128, 2048), BF),
    jax.ShapeDtypeStruct((128, 1024), BF),
    jax.ShapeDtypeStruct((128, 1024), BF),
    jax.ShapeDtypeStruct((128, 1024), BF),
    jax.ShapeDtypeStruct((16, 2048), F32),
)


def layer(tables, q, k, v, grad, weight):
    anywhere = pl.BlockSpec(memory_space=pl.ANY)
    dma = pltpu.SemaphoreType.DMA
    vm = pltpu.VMEM
    return pl.pallas_call(
        layer_kernel,
        out_shape=OUTPUTS,
        in_specs=[pl.BlockSpec(memory_space=pltpu.SMEM)] + [anywhere] * 5,
        out_specs=(anywhere,) * 5,
        scratch_shapes=[
            vm((2, BLK, 1024), BF),
            vm((2, BLK, 1024), BF),
            vm((2, BLK, 1024), BF),
            vm((128, 2048), BF),
            vm((1024, 2048), BF),
            vm((2, BLK, 1024), BF),
            vm((256, BLK, HD), BF),
            vm((16, BLK, HD), BF),
            vm((16, BLK, HD), BF),
            vm((1024, 512), F32),
            vm((1024, HD), BF),
            vm((1024, HD), BF),
            vm((128, 1024), BF),
            vm((129, BLK, HD), F32),
            vm((129, BLK, HD), F32),
            vm((4, 2, 8, 128, HD), BF),
            vm((4, 2, 8, 128, HD), BF),
            vm((4, 2, 8, 128, HD), BF),
            vm((2, 2, 8, 128, HD), BF),
            vm((2, 2, 4, 128, HD), BF),
            vm((2, 8, 128, HD), BF),
            vm((2, 2, 4, 32, 16, 256), BF),
            vm((2, 4, 32, 16, 256), BF),
            vm((2, 2, 16, 16, 256), BF),
            vm((2, 2, 32, 16, 256), BF),
            vm((2, 32, 16, 256), BF),
            vm((2, 4, 8, 16, 256), BF),
            vm((8, 16, 512), BF),
            vm((8, 16, 512), BF),
            vm((16, 512), F32),
            vm((128, 2048), BF),
            vm((1024, 128), BF),
            vm((16, 2048), F32),
            dma((7,)),
            dma((8,)),
            dma((6,)),
            dma((10,)),
            dma((2, 7)),
            dma((2, 8, 3)),
            dma((2, 4)),
            dma((2, 6)),
            dma((2, 4)),
            dma((2, 6)),
        ],
        compiler_params=pltpu.CompilerParams(
            collective_id=0, has_side_effects=True, vmem_limit_bytes=63 << 20
        ),
        name="layer",
    )(tables, q, k, v, grad, weight)


def finish_kernel(*refs):
    sources, results, held, sems = refs[:5], refs[5:10], refs[10:15], refs[15]
    taken = [
        pltpu.make_async_copy(src, buf, sems.at[n])
        for n, (src, buf) in enumerate(zip(sources, held))
    ]
    put = [
        pltpu.make_async_copy(buf, dst, sems.at[5 + n])
        for n, (buf, dst) in enumerate(zip(held, results))
    ]
    for copy in taken:
        copy.start()
    for copy, onward in zip(taken, put):
        copy.wait()
        onward.start()
    for copy in put:
        copy.wait()


def finish(arrays):
    anywhere = pl.BlockSpec(memory_space=pl.ANY)
    return pl.pallas_call(
        finish_kernel,
        out_shape=OUTPUTS,
        in_specs=[anywhere] * 5,
        out_specs=(anywhere,) * 5,
        scratch_shapes=[pltpu.VMEM(s.shape, s.dtype) for s in OUTPUTS]
        + [pltpu.SemaphoreType.DMA((10,))],
        compiler_params=pltpu.CompilerParams(vmem_limit_bytes=63 << 20),
        name="finish",
    )(*arrays)


def tables_of(pattern):
    X, Z, C = (lax.axis_index(n) for n in "xzc")
    m = jnp.arange(16, dtype=jnp.int32)
    t = jnp.arange(128, dtype=jnp.int32)
    rows = X * 32 + ((Z + 1 + (m >> 1)) & 7) * 4 + C * 2 + (m & 1)
    chosen = rows[None, :, None] == t[None, None, :]
    mine = jnp.sum(jnp.where(chosen, pattern.T[:, None, :], 0), axis=2).reshape(128)
    s = mine >> 1
    places = ((s & 1) * 4 + (s >> 4)) * 32 + ((s >> 1) & 7) * 2 + (mine & 1)
    order = (t & 15) * 8 + (t >> 4)
    same = mine[None, :] == mine[:, None]
    earlier = order[None, :] < order[:, None]
    before = jnp.max(jnp.where(same & earlier, order[None, :], -1), axis=1)
    last = jnp.max(jnp.where(mine[None, :] == t[:, None], order[None, :], -1), axis=1)
    links = jnp.stack([before, last])
    links = jnp.where(links < 0, 128, (links & 7) * 16 + (links >> 3))
    return jnp.concatenate([places[None], links])


def local(query_in, key_in, value_in, out_weight, grad_out, pattern):
    results = layer(
        tables_of(pattern),
        *(a.reshape(2, BLK, 1024) for a in (query_in, key_in, value_in)),
        grad_out[0],
        out_weight,
    )
    mixed_out, query_grad, key_grad, value_grad, weight_grad = finish(results)
    return (mixed_out[None], query_grad[None], key_grad[None], value_grad[None], weight_grad)


def solution(mesh):
    devices = mesh.devices.reshape(4, 8, 2, 4)
    inner = Mesh(devices, ("x", "z", "c", "rep"))
    seq = ("x", "z", "c")
    rows = P("rep", seq, None)
    return jax.shard_map(
        local,
        mesh=inner,
        in_specs=(rows, rows, rows, P(), rows, P()),
        out_specs=(rows, rows, rows, rows, P(seq, None)),
        check_vma=False,
    )
```
